32 devices in a mesh: row: 8 (over z, y), col: 4 (over x, core).
Axes of the slice: x: 2, y: 2, z: 4, core: 2. Of those that a mesh axis runs over, the one named last changes fastest.
Arguments:
- leaf_inverse: bfloat16 [32, 1024, 1024], P(('row', 'col')), as said below
- leaf_rhs: bfloat16 [32, 1024, 512], P(('row', 'col')), may hold values from -6 to 6
- leaf_tiles: bfloat16 [32, 1024, 1024], P(('row', 'col')), may hold values from -0.09375 to 0.09375
- mid_inverse_t: bfloat16 [8, 1024, 1024], P('col', None, 'row'), as said below
- mid_rhs: bfloat16 [8, 1024, 512], P('col', 'row'), may hold values from -6 to 6
- mid_tiles: bfloat16 [8, 1024, 1024], P('col', None, 'row'), may hold values from -0.125 to 0.125
- top_inverse_t: bfloat16 [2, 1024, 1024], P(None, None, 'col'), as said below
- top_rhs: bfloat16 [2, 1024, 512], P(None, 'col'), may hold values from -6 to 6
- tile_lists: int32 [32, 1], P(('row', 'col')), may hold values from 0 to 1
Outputs:
- leaf_solved: bfloat16 [32, 1024, 512], P(('row', 'col'))
- mid_solved: bfloat16 [8, 1024, 512], P('col', 'row')
- top_solved: bfloat16 [2, 1024, 512], P(None, 'col')
The draws below stay inside these ranges and needn't reach their ends.
Inputs may be any that keep to these rules, and one draw needn't show every extreme that they name: Each leaf_inverse[d] is zero above its diagonal and has diagonal entries between 0.75 and 1.25. Each mid_inverse_t[q] is zero below its diagonal and has diagonal entries between 0.75 and 1.25. Each top_inverse_t[b] is zero below its diagonal and has diagonal entries between 0.75 and 1.25.
All inputs are finite; a program needn't handle non-finite values.
Results may differ from the reference program's by a relative error of at most 0.0065.
Values may be sent and summed in bfloat16 or wider, within the bound.
No kernel may reach another device: no remote copies, remote signals or barrier semaphores. Data moves between devices by JAX's collectives and lax.ppermute only.
A program may use at most 64 MiB of HBM per device.

```python
import math
import jax
import jax.numpy as jnp
from jax import lax

W = 1024
SRC = 512
NB = 2
LEAVES = 32
MID = 8
TOP = 2
N_ROW = 8
N_COL = 4


def triangle(key, number):
    jitter_key, diagonal_key = jax.random.split(key)
    jitter = jnp.clip(jax.random.normal(jitter_key, (number, W, W), jnp.float32), -4.0, 4.0)
    strict_lower = jnp.tril(jnp.ones((W, W), jnp.float32), -1)
    diagonal = jax.random.uniform(diagonal_key, (number, W), jnp.float32, 0.75, 1.25)
    return jitter * strict_lower * (0.8 / math.sqrt(W)) + diagonal[:, :, None] * jnp.eye(W, dtype=jnp.float32)


def draw_leaf_inverse(key, part):
    return triangle(jax.random.fold_in(key, 11), LEAVES).astype(jnp.bfloat16)


def draw_mid_inverse_t(key, part):
    return jnp.swapaxes(triangle(jax.random.fold_in(key, 12), MID), 1, 2).astype(jnp.bfloat16)


def draw_top_inverse_t(key, part):
    return jnp.swapaxes(triangle(jax.random.fold_in(key, 13), TOP), 1, 2).astype(jnp.bfloat16)


def place_ends(result, rng, least, high):
    spot = [jax.random.randint(jax.random.fold_in(rng, axis), (), 0, length) for axis, length in enumerate(result.shape)]
    main_axis = result.shape.index(max(result.shape))
    next_to = spot[:main_axis] + [(spot[main_axis] + 1) % result.shape[main_axis]] + spot[main_axis + 1:]
    return result.at[tuple(spot)].set(least).at[tuple(next_to)].set(high)


def spiked(drawn, stream_key, source, target, blocks, factor):
    def block_of(axis_at):
        return (jnp.arange(drawn.shape[axis_at]) // (drawn.shape[axis_at] // blocks)).reshape((-1,) + (1,) * (drawn.ndim - 1 - axis_at))

    first = jax.random.permutation(stream_key, blocks)[block_of(target)]
    second = (block_of(target) + blocks // 2) % blocks
    return jnp.where((block_of(source) == first) | (block_of(source) == second), factor * drawn, drawn)


def level_of(rng, dims, cuts, least, high):
    factor_of, own = 1.0, jax.random.fold_in(rng, 6)
    for position, shards_of in cuts:
        steps = jnp.exp(jax.random.uniform(jax.random.fold_in(own, position), (shards_of,), jnp.float32, least / len(cuts), high / len(cuts)))
        factor_of = factor_of * jnp.repeat(steps, dims[position] // shards_of).reshape([-1 if axis == position else 1 for axis in range(len(dims))])
    return factor_of


def scatter_about(rng, dims, width, reach, cuts=(), kind=jnp.bfloat16):
    values = width * jax.random.normal(rng, dims, jnp.float32)
    if cuts:
        values = values * level_of(rng, dims, cuts, -0.22, 0.18)
    return jnp.clip(values, -reach, reach).astype(kind)


def bell_draw_with(stream_key, shape, scale, limit, cuts, heavy, kind=jnp.bfloat16):
    entries = scale * jax.random.normal(stream_key, shape, jnp.float32)
    if cuts:
        entries = entries * level_of(stream_key, shape, cuts, -0.22, 0.18)
    return jnp.clip(spiked(entries, jax.random.fold_in(stream_key, 3), *heavy), -limit, limit).astype(kind)


def setup_inputs(seed: int = 0) -> dict:
    arg_keys = jax.random.split(jax.random.key(seed), 10)
    return {
        "leaf_inverse": draw_leaf_inverse(jax.random.fold_in(arg_keys[9], 71), 0),
        "leaf_rhs": scatter_about(arg_keys[1], (LEAVES, W, SRC), 1.0, 6.0, ((0, 32),)),
        "leaf_tiles": scatter_about(arg_keys[2], (LEAVES, W, W), (W * N_ROW // NB) ** -0.5, 0.09375, ((0, 32),)),
        "mid_inverse_t": draw_mid_inverse_t(jax.random.fold_in(arg_keys[9], 71), 0),
        "mid_rhs": scatter_about(arg_keys[4], (MID, W, SRC), 1.0, 6.0, ((0, 4), (1, 8))),
        "mid_tiles": bell_draw_with(arg_keys[5], (MID, W, W), (W * N_COL) ** -0.5, 0.125, ((0, 4), (2, 8)), (2, 1, 8, 2.0)),
        "top_inverse_t": draw_top_inverse_t(jax.random.fold_in(arg_keys[9], 71), 0),
        "top_rhs": scatter_about(arg_keys[7], (TOP, W, SRC), 1.0, 6.0, ((1, 4),)),
        "tile_lists": place_ends(jax.random.randint(arg_keys[8], (LEAVES, 1), 0, NB), jax.random.fold_in(arg_keys[8], 1), 0, NB - 1).astype(jnp.int32),
    }


def reference(leaf_inverse, leaf_rhs, leaf_tiles, mid_inverse_t, mid_rhs, mid_tiles, top_inverse_t, top_rhs, tile_lists):
    def leaf_sweep(running, leaf_index):
        solved = jnp.dot(leaf_inverse[leaf_index], leaf_rhs[leaf_index], preferred_element_type=jnp.float32).astype(jnp.bfloat16)
        update = jnp.dot(leaf_tiles[leaf_index], solved, preferred_element_type=jnp.float32)
        target = ((leaf_index % N_COL) * NB + tile_lists[leaf_index, 0]).astype(jnp.int32)
        return running.at[target].add(update), solved

    leaf_ids = jnp.arange(LEAVES, dtype=jnp.int32)
    mid_update, leaf_solved = lax.scan(leaf_sweep, jnp.zeros((MID, W, SRC), jnp.float32), leaf_ids)
    mid_resid = (mid_rhs.astype(jnp.float32) - mid_update).astype(jnp.bfloat16)
    mid_solved = jnp.einsum("qjw,qjs->qws", mid_inverse_t.astype(jnp.float32), mid_resid.astype(jnp.float32)).astype(jnp.bfloat16)

    tiles_grid = mid_tiles.reshape(N_COL, NB, W, W).astype(jnp.float32)
    solved_grid = mid_solved.reshape(N_COL, NB, W, SRC).astype(jnp.float32)
    top_update = jnp.einsum("cbij,cbjs->bis", tiles_grid, solved_grid)
    top_resid = (top_rhs.astype(jnp.float32) - top_update).astype(jnp.bfloat16)
    top_solved = jnp.einsum("bjw,bjs->bws", top_inverse_t.astype(jnp.float32), top_resid.astype(jnp.float32)).astype(jnp.bfloat16)
    return leaf_solved, mid_solved, top_solved
```

```python
import jax
import jax.numpy as jnp
from jax import lax
from jax.sharding import PartitionSpec as P

CORES = 2


F32, BF16 = jnp.float32, jnp.bfloat16


def wide(x):
    return x.astype(F32)


def total(terms):
    acc = terms[0]
    for term in terms[1:]:
        acc = acc + term
    return acc


def take(x, index, axis=0):
    return lax.dynamic_index_in_dim(x, index, axis, keepdims=False)


def make_local(n_row, n_col):
    n_x = n_col // CORES

    def shift(x, k):
        return lax.ppermute(x, "row", [(i, (i + k) % n_row) for i in range(n_row)])

    def local(
        leaf_inverse,
        leaf_rhs,
        leaf_tiles,
        mid_inverse_t,
        mid_rhs,
        mid_tiles,
        top_inverse_t,
        top_rhs,
        tile_lists,
    ):
        nb, depth, own_rows = mid_inverse_t.shape
        n_top, _, own_top = top_inverse_t.shape
        src = leaf_rhs.shape[2]
        row, col = lax.axis_index("row"), lax.axis_index("col")
        n_z = n_row // n_top
        z, y = row // n_top, row % n_top
        x, core = col // CORES, col % CORES

        slots = tile_lists[0]
        have = 1
        while have < n_row:
            more = min(have, n_row - have)
            slots = jnp.concatenate([slots, shift(slots[:more], have)])
            have += more

        solved_leaf = jnp.dot(
            leaf_inverse[0], leaf_rhs[0], preferred_element_type=F32
        ).astype(BF16)
        update = jnp.dot(leaf_tiles[0], solved_leaf, preferred_element_type=F32).astype(BF16)
        update = update.reshape(n_row, own_rows, src)

        terms = [take(update, row)]
        for k in range(1, n_row):
            terms.append(shift(take(update, (row + k) % n_row), k))
        resid = []
        for s in range(nb):
            picked = [jnp.where(slots[k] == s, wide(t), 0.0) for k, t in enumerate(terms)]
            resid.append((wide(mid_rhs[s]) - total(picked)).astype(BF16))
        resid = jnp.stack(resid)

        ring = list(range(0, n_row, 2)) + list(range(1, n_row, 2))[::-1]
        place = [ring.index(i) for i in range(n_row)]
        forth = [(ring[i], ring[(i + 1) % n_row]) for i in range(n_row)]
        back = [(b, a) for a, b in forth]
        spot = jnp.asarray(place, jnp.int32)[row]
        inverse_blocks = mid_inverse_t.reshape(nb, n_row, own_rows, own_rows)

        def partial_solve(block, step, lanes):
            owner = jnp.asarray(ring, jnp.int32)[(spot + step) % n_row]
            part = take(inverse_blocks, owner, 1)[lanes]
            return lax.dot_general(
                part, block, (((1,), (1,)), ((0,), (0,))), preferred_element_type=F32
            )

        everything = slice(None)
        solved = partial_solve(resid, 0, everything)
        f = b = resid
        for step in range(1, (n_row - 1) // 2 + 1):
            f = lax.ppermute(f, "row", forth)
            b = lax.ppermute(b, "row", back)
            solved = solved + partial_solve(f, -step, everything)
            solved = solved + partial_solve(b, step, everything)
        half = nb // 2
        f = lax.ppermute(f[:half], "row", forth)
        b = lax.ppermute(b[half:], "row", back)
        last = n_row // 2
        solved = solved + jnp.concatenate(
            [partial_solve(f, -last, slice(0, half)), partial_solve(b, last, slice(half, nb))]
        )
        mid_own = solved.astype(BF16)

        tiles = mid_tiles.reshape(nb, n_x, CORES, own_top, own_rows)

        def top_terms(core_index):
            return lax.dot_general(
                take(tiles, core_index, 2),
                mid_own,
                (((3,), (1,)), ((0,), (0,))),
                preferred_element_type=F32,
            )

        other = [(i, i ^ 1) for i in range(n_col)]
        got = lax.ppermute(top_terms(1 - core).astype(BF16), "col", other)
        part = (top_terms(core) + wide(got)).astype(BF16)

        def square(i, dx, dy):
            r, c = divmod(i, n_col)
            zz, yy = divmod(r, n_top)
            xx, cc = divmod(c, CORES)
            return (zz * n_top + (yy + dy) % n_top) * n_col + ((xx + dx) % n_x) * CORES + cc

        terms = []
        for dx in reversed(range(n_x)):
            for dy in reversed(range(n_top)):
                piece = take(take(part, (y + dy) % n_top), (x + dx) % n_x)
                if dx or dy:
                    piece = lax.ppermute(
                        piece,
                        ("row", "col"),
                        [(i, square(i, dx, dy)) for i in range(n_row * n_col)],
                    )
                terms.append(wide(piece))
        part = total(terms[::-1]).astype(BF16)

        width = src // n_z
        terms = []
        for dz in range(n_z):
            piece = lax.dynamic_slice_in_dim(part, ((z + dz) % n_z) * width, width, 1)
            if dz:
                piece = shift(piece, dz * n_top)
            terms.append(wide(piece))
        own_rhs = lax.dynamic_slice_in_dim(take(top_rhs, y), z * width, width, 1)
        top_resid = (wide(own_rhs) - total(terms)).astype(BF16)

        inverse = take(top_inverse_t, y).reshape(n_col, own_top, own_top)
        solved = None
        for dc in range(n_col):
            piece = top_resid
            if dc:
                piece = lax.ppermute(
                    top_resid, "col", [(i, i ^ dc) for i in range(n_col)]
                )
            term = lax.dot_general(
                take(inverse, col ^ dc),
                piece,
                (((0,), (0,)), ((), ())),
                preferred_element_type=F32,
            )
            solved = term if solved is None else solved + term
        mine = solved.astype(BF16)

        top_own = jnp.zeros((n_row, own_top, width), BF16)
        for k in range(n_row):
            piece = shift(mine, k) if k else mine
            top_own = lax.dynamic_update_index_in_dim(
                top_own, piece, (row - k) % n_row, 0
            )
        top_own = (
            top_own.reshape(n_z, n_top, own_top, width)
            .transpose(1, 2, 0, 3)
            .reshape(n_top, own_top, src)
        )
        return solved_leaf[None], mid_own, top_own

    return local


def solution(mesh):
    placed = (
        P(("row", "col"), None, None),
        P(("row", "col"), None, None),
        P(("row", "col"), None, None),
        P("col", None, "row"),
        P("col", "row", None),
        P("col", None, "row"),
        P(None, None, "col"),
        P(None, "col", None),
        P(("row", "col"), None),
    )
    return jax.shard_map(
        make_local(mesh.shape["row"], mesh.shape["col"]),
        mesh=mesh,
        in_specs=placed,
        out_specs=(P(("row", "col"), None, None), P("col", "row", None), P(None, "col", None)),
        check_vma=False,
    )
```

```python
import jax
import jax.numpy as jnp
from jax import lax
from jax.experimental import pallas as pl
from jax.experimental.pallas import tpu as pltpu
from jax.sharding import PartitionSpec as P

CORES = 2
MARK = 16
LANES = 128


F32, BF16 = jnp.float32, jnp.bfloat16
VMEM = pl.BlockSpec(memory_space=pltpu.VMEM)
SMEM = pl.BlockSpec(memory_space=pltpu.SMEM)


def wide(x):
    return x.astype(F32)


def total(terms):
    acc = terms[0]
    for term in terms[1:]:
        acc = acc + term
    return acc


def dot(a, b, a_dim):
    return lax.dot_general(a, b, (((a_dim,), (0,)), ((), ())), preferred_element_type=F32)


def call(body, name, shapes, args, specs=None, scratch=()):
    return pl.pallas_call(
        body,
        name=name,
        out_shape=[jax.ShapeDtypeStruct(s, BF16) for s in shapes],
        in_specs=specs or [VMEM] * len(args),
        out_specs=[VMEM] * len(shapes),
        scratch_shapes=scratch,
    )(*args)


def leaf_stage(leaf_inverse, leaf_rhs, leaf_tiles, tile_lists, n_row):
    depth, src = leaf_rhs.shape
    rows = depth // n_row
    chunks = src // LANES
    step = min(256, depth)

    def body(inverse, rhs, tiles, slot, solved, *rest):
        blocks, update = rest[:n_row], rest[n_row]
        row = lax.axis_index("row")
        for i in range(0, depth, step):
            block = dot(inverse[i : i + step, : i + step], rhs[: i + step, :], 1)
            solved[i : i + step, :] = block.astype(BF16)
        for i in range(0, depth, step):
            update[i : i + step, :] = dot(tiles[i : i + step, :], solved[...], 1).astype(BF16)
        mark = jnp.full((MARK, LANES), slot[0, 0].astype(F32), F32).astype(BF16)
        for k in range(n_row):
            at = pl.ds(pl.multiple_of((row ^ k) * rows, rows), rows)
            for j in range(chunks):
                lanes = slice(j * LANES, (j + 1) * LANES)
                blocks[k][j * rows : (j + 1) * rows, :] = update[at, lanes]
            blocks[k][chunks * rows :, :] = mark

    out = call(
        body,
        "leaf",
        [(depth, src)] + [(chunks * rows + MARK, LANES)] * n_row,
        (leaf_inverse, leaf_rhs, leaf_tiles, tile_lists),
        [VMEM, VMEM, VMEM, SMEM],
        [pltpu.VMEM((depth, src), BF16)],
    )
    return out[0], out[1:]


def slot_sums(blocks, nb, rows, chunk):
    sums = [None] * nb
    for ref in blocks:
        value = wide(ref[chunk * rows : (chunk + 1) * rows, :])
        mark = wide(ref[ref.shape[0] - MARK : ref.shape[0] - MARK + 1, :])
        for s in range(nb):
            term = jnp.where(mark == float(s), value, 0.0)
            sums[s] = term if sums[s] is None else sums[s] + term
    return sums


def cross_stage(blocks, nb, rows, src):
    def body(*refs):
        outs = refs[len(blocks) :]
        for j in range(src // LANES):
            sums = slot_sums(refs[: len(blocks)], nb, rows, j)
            for s in range(nb):
                outs[0][s * rows : (s + 1) * rows, j * LANES : (j + 1) * LANES] = sums[s].astype(
                    BF16
                )

    return call(body, "cross", [(nb * rows, src)], tuple(blocks))[0]


def resid_stage(blocks, crossed, mid_rhs):
    nb, rows, src = mid_rhs.shape

    def body(*refs):
        near = refs[: len(blocks)]
        far, rhs = refs[len(blocks) : len(blocks) + 2]
        outs = refs[len(blocks) + 2 :]
        for j in range(src // LANES):
            lanes = slice(j * LANES, (j + 1) * LANES)
            sums = slot_sums(near, nb, rows, j)
            for s in range(nb):
                update = sums[s] + wide(far[s * rows : (s + 1) * rows, lanes])
                outs[s][:, lanes] = (wide(rhs[s, :, lanes]) - update).astype(BF16)

    return call(body, "resid", [(rows, src)] * nb, (*blocks, crossed, mid_rhs))


def mid_stage(blocks, steps, mid_inverse_t, mid_tiles, n_row, n_x, own_top):
    nb, depth, rows = mid_inverse_t.shape
    src = blocks[0][0].shape[1]
    count = len(steps)

    def body(*refs):
        parts, (inverse, tiles, own, sent) = refs[: nb * count], refs[nb * count :]
        row, core = lax.axis_index("row"), lax.axis_index("col") % CORES
        spot = jnp.where(row % 2 == 0, row // 2, n_row - 1 - row // 2)
        for q in range(nb):
            acc = None
            for i, step in enumerate(steps):
                at = (spot + step + n_row) % n_row
                owner = jnp.where(at < n_row // 2, 2 * at, 2 * (n_row - 1 - at) + 1)
                start = pl.multiple_of(owner * rows, rows)
                term = dot(inverse[q, pl.ds(start, rows), :], parts[q * count + i][...], 0)
                acc = term if acc is None else acc + term
            own[q] = acc.astype(BF16)
        for q in range(nb):
            for x in range(n_x):
                start = pl.multiple_of((x * CORES + 1 - core) * own_top, own_top)
                block = dot(tiles[q, pl.ds(start, own_top), :], own[q], 1)
                sent[q, x] = block.astype(BF16)

    return call(
        body,
        "mid",
        [(nb, rows, src), (nb, n_x, own_top, src)],
        (*[b for per_q in blocks for b in per_q], mid_inverse_t, mid_tiles),
    )


def core_stage(mid_own, mid_tiles, got, own_top):
    nb, n_x, _, src = got.shape

    def body(own, tiles, other, *pieces):
        row, col = lax.axis_index("row"), lax.axis_index("col")
        y, x, core = row % nb, col // CORES, col % CORES
        for dx in range(n_x):
            for dy in range(nb):
                xx, q = x ^ dx, y ^ dy
                start = pl.multiple_of((xx * CORES + core) * own_top, own_top)
                block = dot(tiles[q, pl.ds(start, own_top), :], own[q], 1)
                pieces[dx * nb + dy][...] = (block + wide(other[q, xx])).astype(BF16)

    return call(body, "core", [(own_top, src)] * (n_x * nb), (mid_own, mid_tiles, got))


def square_stage(pieces, n_z, n_top):
    rows, src = pieces[0].shape
    width = src // n_z

    def body(*refs):
        outs = refs[len(pieces) :]
        z = lax.axis_index("row") // n_top
        for k in range(n_z):
            lanes = pl.ds(pl.multiple_of((z ^ k) * width, width), width)
            outs[k][...] = total([wide(ref[:, lanes]) for ref in refs[: len(pieces)]]).astype(BF16)

    return call(body, "square", [(rows, width)] * n_z, tuple(pieces))


def top_resid_stage(pieces, top_rhs):
    n_top, rows, _ = top_rhs.shape
    width = pieces[0].shape[1]

    def body(*refs):
        rhs, out = refs[len(pieces) :]
        row = lax.axis_index("row")
        z, y = row // n_top, row % n_top
        lanes = pl.ds(pl.multiple_of(z * width, width), width)
        out[...] = (wide(rhs[y, :, lanes]) - total([wide(r[...]) for r in refs[: len(pieces)]])).astype(
            BF16
        )

    return call(body, "top_resid", [(rows, width)], (*pieces, top_rhs))[0]


def top_solve_stage(pieces, top_inverse_t):
    n_top, _, rows = top_inverse_t.shape
    width = pieces[0].shape[1]

    def body(*refs):
        inverse, out = refs[len(pieces) :]
        y, col = lax.axis_index("row") % n_top, lax.axis_index("col")
        acc = None
        for k, ref in enumerate(refs[: len(pieces)]):
            start = pl.multiple_of((col ^ k) * rows, rows)
            term = dot(inverse[y, pl.ds(start, rows), :], ref[...], 0)
            acc = term if acc is None else acc + term
        out[...] = acc.astype(BF16)

    return call(body, "top_solve", [(rows, width)], (*pieces, top_inverse_t))[0]


def spread_stage(pieces, n_z, n_top):
    rows, width = pieces[0].shape

    def body(*refs):
        out = refs[len(pieces)]
        row = lax.axis_index("row")
        for k, ref in enumerate(refs[: len(pieces)]):
            z, y = (row ^ k) // n_top, (row ^ k) % n_top
            out[y, :, pl.ds(pl.multiple_of(z * width, width), width)] = ref[...]

    return call(body, "spread", [(n_top, rows, n_z * width)], tuple(pieces))[0]


def take(x, index, axis=0):
    return lax.dynamic_index_in_dim(x, index, axis, keepdims=False)


def narrow_square(pieces, n_z, n_top):
    width = pieces[0].shape[1] // n_z
    z = lax.axis_index("row") // n_top
    whole = total([wide(p) for p in pieces]).astype(BF16)
    return [lax.dynamic_slice_in_dim(whole, (z ^ k) * width, width, 1) for k in range(n_z)]


def narrow_top_resid(pieces, top_rhs):
    row = lax.axis_index("row")
    n_top, width = top_rhs.shape[0], pieces[0].shape[1]
    rhs = lax.dynamic_slice_in_dim(take(top_rhs, row % n_top), row // n_top * width, width, 1)
    return (wide(rhs) - total([wide(p) for p in pieces])).astype(BF16)


def narrow_top_solve(pieces, top_inverse_t):
    n_top, _, rows = top_inverse_t.shape
    col = lax.axis_index("col")
    inverse = take(top_inverse_t, lax.axis_index("row") % n_top)
    terms = [
        dot(lax.dynamic_slice_in_dim(inverse, (col ^ k) * rows, rows, 0), p, 0)
        for k, p in enumerate(pieces)
    ]
    return total(terms).astype(BF16)


def narrow_spread(pieces, n_z, n_top):
    rows, width = pieces[0].shape
    row = lax.axis_index("row")
    out = jnp.zeros((n_z * n_top, rows, width), BF16)
    for k, piece in enumerate(pieces):
        out = lax.dynamic_update_index_in_dim(out, piece, row ^ k, 0)
    out = out.reshape(n_z, n_top, rows, width).transpose(1, 2, 0, 3)
    return out.reshape(n_top, rows, n_z * width)


def make_local(n_row, n_col):
    n_x = n_col // CORES
    half = n_row // 2

    def row_xor(x, k):
        return lax.ppermute(x, "row", [(i, i ^ k) for i in range(n_row)])

    def col_xor(x, k):
        return lax.ppermute(x, "col", [(i, i ^ k) for i in range(n_col)])

    def both_xor(x, k, c):
        return lax.ppermute(
            x,
            ("row", "col"),
            [
                (i, (i // n_col ^ k) * n_col + (i % n_col ^ c))
                for i in range(n_row * n_col)
            ],
        )

    ring = list(range(0, n_row, 2)) + list(range(1, n_row, 2))[::-1]
    forth = [(ring[i], ring[(i + 1) % n_row]) for i in range(n_row)]
    back = [(b, a) for a, b in forth]

    def local(
        leaf_inverse,
        leaf_rhs,
        leaf_tiles,
        mid_inverse_t,
        mid_rhs,
        mid_tiles,
        top_inverse_t,
        top_rhs,
        tile_lists,
    ):
        nb, _, own_rows = mid_inverse_t.shape
        n_top, _, own_top = top_inverse_t.shape
        src = leaf_rhs.shape[2]
        n_z = n_row // n_top

        solved_leaf, update = leaf_stage(
            leaf_inverse[0], leaf_rhs[0], leaf_tiles[0], tile_lists, n_row
        )

        crossing = [update[half]] + [row_xor(update[half + k], k) for k in range(1, half)]
        staying = [update[0]] + [row_xor(update[k], k) for k in range(1, half)]
        crossed = row_xor(cross_stage(crossing, nb, own_rows, src), half)
        resid = resid_stage(staying, crossed, mid_rhs)

        blocks, steps = [[r] for r in resid], [0]
        ahead, behind = list(resid), list(resid)
        for step in range(1, half):
            for q in range(nb):
                ahead[q] = lax.ppermute(ahead[q], "row", forth)
                behind[q] = lax.ppermute(behind[q], "row", back)
                blocks[q] += [ahead[q], behind[q]]
            steps += [-step, step]
        for q in range(nb):
            if q < nb // 2:
                blocks[q].append(lax.ppermute(ahead[q], "row", forth))
            else:
                blocks[q].append(lax.ppermute(behind[q], "row", back))
        steps.append(half)
        mid_own, sent = mid_stage(
            blocks, steps, mid_inverse_t, mid_tiles, n_row, n_x, own_top
        )

        pieces = core_stage(mid_own, mid_tiles, col_xor(sent, 1), own_top)
        got = [pieces[0]]
        for dx in reversed(range(n_x)):
            for dy in reversed(range(n_top)):
                if dx or dy:
                    got.append(both_xor(pieces[dx * n_top + dy], dy, dx * CORES))
        dense = src // n_z % LANES == 0
        square, top_resid, top_solve, spread = (
            (square_stage, top_resid_stage, top_solve_stage, spread_stage)
            if dense
            else (narrow_square, narrow_top_resid, narrow_top_solve, narrow_spread)
        )
        pieces = square(got, n_z, n_top)
        got = [pieces[0]] + [row_xor(pieces[k], k * n_top) for k in range(1, n_z)]
        own = top_resid(got, top_rhs)

        mine = top_solve([own] + [col_xor(own, k) for k in range(1, n_col)], top_inverse_t)
        top_own = spread([mine] + [row_xor(mine, k) for k in range(1, n_row)], n_z, n_top)
        return solved_leaf[None], mid_own, top_own

    return local


def solution(mesh):
    placed = (
        P(("row", "col"), None, None),
        P(("row", "col"), None, None),
        P(("row", "col"), None, None),
        P("col", None, "row"),
        P("col", "row", None),
        P("col", None, "row"),
        P(None, None, "col"),
        P(None, "col", None),
        P(("row", "col"), None),
    )
    return jax.shard_map(
        make_local(mesh.shape["row"], mesh.shape["col"]),
        mesh=mesh,
        in_specs=placed,
        out_specs=(P(("row", "col"), None, None), P("col", "row", None), P(None, "col", None)),
        check_vma=False,
    )
```

```python
import jax
import jax.numpy as jnp
from jax import lax
from jax.experimental import pallas as pl
from jax.experimental.pallas import tpu as pltpu
from jax.sharding import PartitionSpec as P


CORES = 2
MARK = 16
LANES = 128


F32, BF16 = jnp.float32, jnp.bfloat16
VMEM = pl.BlockSpec(memory_space=pltpu.VMEM)
SMEM = pl.BlockSpec(memory_space=pltpu.SMEM)
HBM = pl.BlockSpec(memory_space=pltpu.HBM)


def wide(x):
    return x.astype(F32)


def total(terms):
    acc = terms[0]
    for term in terms[1:]:
        acc = acc + term
    return acc


def dot(a, b, a_dim):
    return lax.dot_general(a, b, (((a_dim,), (0,)), ((), ())), preferred_element_type=F32)


def in_hbm(x):
    return pltpu.with_memory_space_constraint(x, pltpu.HBM)


def call(body, shapes, args, specs=None, scratch=(), out_specs=None):
    return pl.pallas_call(
        body,
        out_shape=[jax.ShapeDtypeStruct(s, BF16) for s in shapes],
        in_specs=specs or [VMEM] * len(args),
        out_specs=out_specs or [VMEM] * len(shapes),
        scratch_shapes=scratch,
        compiler_params=pltpu.CompilerParams(vmem_limit_bytes=16 << 20),
    )(*args)


def leaf_stage(leaf_inverse, leaf_rhs, leaf_tiles, tile_lists, mid_inverse_t, mid_tiles, n_row):
    nb, _, own_rows = mid_inverse_t.shape
    depth, src = leaf_rhs.shape
    rows = depth // n_row
    chunks = src // LANES
    step = min(256, depth)

    count = depth // step

    def body(inverse_hbm, rhs_hbm, tiles_hbm, slot, mid_inverse, mid_tile, solved_hbm, swap, *rest):
        blocks = rest[:n_row]
        inverse, rhs, tiles, solved, update, sems = rest[n_row:]
        row = lax.axis_index("row")
        spans = [slice(i * step, (i + 1) * step) for i in range(count)]

        def fetch(source, target, sem, *at):
            copy = pltpu.make_async_copy(source.at[at], target.at[at], sem)
            copy.start()
            return copy

        first, second = [], []
        for i, span in enumerate(spans):
            first.append(fetch(rhs_hbm, rhs, sems.at[0, i], span))
            first.append(
                fetch(inverse_hbm, inverse, sems.at[1, i], span, slice(0, (i + 1) * step))
            )
        for i, span in enumerate(spans):
            second.append(fetch(tiles_hbm, tiles, sems.at[2, i], span))
        stored = []
        for i, source in enumerate((mid_inverse, mid_tile)):
            copy = pltpu.make_async_copy(source.at[1 - row % nb], swap.at[i], sems.at[4, i])
            copy.start()
            stored.append(copy)
        for i, span in enumerate(spans):
            first[2 * i].wait()
            first[2 * i + 1].wait()
            block = dot(inverse[span, : (i + 1) * step], rhs[: (i + 1) * step, :], 1)
            solved[span, :] = block.astype(BF16)
            copy = pltpu.make_async_copy(solved.at[span], solved_hbm.at[span], sems.at[3, i])
            copy.start()
            stored.append(copy)
        for i, span in enumerate(spans):
            second[i].wait()
            update[span, :] = dot(tiles[span, :], solved[...], 1).astype(BF16)
        mark = jnp.full((MARK, LANES), slot[0, 0].astype(F32), F32).astype(BF16)
        for k in range(n_row):
            at = pl.ds(pl.multiple_of((row ^ k) * rows, rows), rows)
            for j in range(chunks):
                lanes = slice(j * LANES, (j + 1) * LANES)
                blocks[k][j * rows : (j + 1) * rows, :] = update[at, lanes]
            blocks[k][chunks * rows :, :] = mark
        for copy in stored:
            copy.wait()

    out = call(
        body,
        [(depth, src), (2, depth, own_rows)] + [(chunks * rows + MARK, LANES)] * n_row,
        (
            *map(in_hbm, (leaf_inverse, leaf_rhs, leaf_tiles)),
            tile_lists,
            *map(in_hbm, (mid_inverse_t, mid_tiles)),
        ),
        [HBM, HBM, HBM, SMEM, HBM, HBM],
        [
            pltpu.VMEM((depth, depth), BF16),
            pltpu.VMEM((depth, src), BF16),
            pltpu.VMEM((depth, depth), BF16),
            pltpu.VMEM((depth, src), BF16),
            pltpu.VMEM((depth, src), BF16),
            pltpu.SemaphoreType.DMA((5, max(count, 2))),
        ],
        [HBM] + [VMEM] * (n_row + 1),
    )
    return out[0], out[1], out[2:]


def slot_sums(blocks, nb, rows, chunk):
    sums = [None] * nb
    for ref in blocks:
        value = wide(ref[chunk * rows : (chunk + 1) * rows, :])
        mark = wide(ref[ref.shape[0] - MARK : ref.shape[0] - MARK + 1, :])
        for s in range(nb):
            term = jnp.where(mark == float(s), value, 0.0)
            sums[s] = term if sums[s] is None else sums[s] + term
    return sums


def cross_stage(blocks, nb, rows, src):
    def body(*refs):
        outs = refs[len(blocks) :]
        for j in range(src // LANES):
            sums = slot_sums(refs[: len(blocks)], nb, rows, j)
            for s in range(nb):
                outs[0][s * rows : (s + 1) * rows, j * LANES : (j + 1) * LANES] = sums[s].astype(
                    BF16
                )

    return call(body, [(nb * rows, src)], tuple(blocks))[0]


def resid_stage(blocks, crossed, mid_rhs):
    nb, rows, src = mid_rhs.shape

    def body(*refs):
        near = refs[: len(blocks)]
        far, rhs, mine, other = refs[len(blocks) :]
        y = lax.axis_index("row") % nb
        for j in range(src // LANES):
            lanes = slice(j * LANES, (j + 1) * LANES)
            sums = slot_sums(near, nb, rows, j)
            first, second = [
                wide(rhs[s, :, lanes])
                - (sums[s] + wide(far[s * rows : (s + 1) * rows, lanes]))
                for s in range(nb)
            ]
            mine[:, lanes] = jnp.where(y == 0, first, second).astype(BF16)
            other[:, lanes] = jnp.where(y == 0, second, first).astype(BF16)

    return call(body, [(rows, src)] * nb, (*blocks, crossed, mid_rhs))


def mid_stage(blocks, mid_inverse_t, mid_tiles, swapped, n_x, own_top):
    nb, _, rows = mid_inverse_t.shape
    src = blocks[0][0].shape[1]
    n_z = len(blocks)

    def body(*refs):
        parts, (inverse, tiles, swap, own, other, sent) = refs[: 2 * n_z], refs[2 * n_z :]
        row, core = lax.axis_index("row"), lax.axis_index("col") % CORES
        z, y = row // nb, row % nb
        acc = None
        for i, ref in enumerate(parts):
            owner = ((z - i // 2 + n_z) % n_z) * nb + (y ^ (i % 2))
            at = pl.ds(pl.multiple_of(owner * rows, rows), rows)
            part = jnp.concatenate([inverse[y, at, :], swap[0, at, :]], axis=1)
            term = dot(part, ref[...], 0)
            acc = term if acc is None else acc + term
        solved = acc.astype(BF16)
        own[...] = solved[:rows]
        other[...] = solved[rows:]
        for x in range(n_x):
            at = pl.ds(pl.multiple_of((x * CORES + 1 - core) * own_top, own_top), own_top)
            part = jnp.concatenate([tiles[y, at, :], swap[1, at, :]], axis=1)
            sent[x] = dot(part, solved, 1).astype(BF16)

    return call(
        body,
        [(rows, src), (rows, src), (n_x, own_top, src)],
        (*[b for pair in blocks for b in pair], mid_inverse_t, mid_tiles, swapped),
    )


def core_stage(own, other, mid_tiles, swapped, got, n_z):
    n_x, own_top, src = got.shape
    nb = mid_tiles.shape[0]
    width = src // n_z
    dense = width % LANES == 0

    def body(own, other, tiles, swap, far, *rest):
        outs, part = (rest[:-1], rest[-1]) if dense else (None, rest[0])
        row, core = lax.axis_index("row"), lax.axis_index("col") % CORES
        z, y = row // nb, row % nb
        solved = jnp.concatenate([own[...], other[...]], axis=0)
        for x in range(n_x):
            at = pl.ds(pl.multiple_of((x * CORES + core) * own_top, own_top), own_top)
            tile = jnp.concatenate([tiles[y, at, :], swap[1, at, :]], axis=1)
            term = dot(tile, solved, 1) + wide(far[x])
            part[x * own_top : (x + 1) * own_top, :] = term.astype(BF16)
        for k in range(n_z if dense else 0):
            lanes = pl.ds(pl.multiple_of((z ^ k) * width, width), width)
            outs[k][...] = part[:, lanes]

    args = (own, other, mid_tiles, swapped, got)
    rows = n_x * own_top
    if dense:
        return call(body, [(rows, width)] * n_z, args, scratch=[pltpu.VMEM((rows, src), BF16)])
    part = call(body, [(rows, src)], args)[0]
    z = lax.axis_index("row") // nb
    return [lax.dynamic_slice_in_dim(part, (z ^ k) * width, width, 1) for k in range(n_z)]


def share_stage(top_rhs, n_z):
    n_top, rows, src = top_rhs.shape
    width = src // n_z
    row = lax.axis_index("row")
    if width % LANES:
        part = lax.dynamic_index_in_dim(top_rhs, row % n_top, 0, keepdims=False)
        return lax.dynamic_slice_in_dim(part, row // n_top * width, width, 1)

    def body(rhs, out):
        row = lax.axis_index("row")
        lanes = pl.ds(pl.multiple_of(row // n_top * width, width), width)
        out[...] = rhs[row % n_top, :, lanes]

    return call(body, [(rows, width)], (top_rhs,))[0]


def sum_stage(pieces):
    def body(*refs):
        refs[-1][...] = total([wide(ref[...]) for ref in refs[:-1]]).astype(BF16)

    return call(body, [pieces[0].shape], tuple(pieces))[0]


def top_resid_stage(pieces, shares):
    n_x = len(shares)
    rows, width = shares[0].shape

    def body(*refs):
        terms, rhs, out = refs[: len(pieces)], refs[len(pieces) : -1], refs[-1]
        x = lax.axis_index("col") // CORES
        for dx in range(n_x):
            at = pl.ds(pl.multiple_of((x ^ dx) * rows, rows), rows)
            update = total([wide(ref[at, :]) for ref in terms])
            out[at, :] = (wide(rhs[dx][...]) - update).astype(BF16)

    return call(body, [(n_x * rows, width)], (*pieces, *shares))[0]


def top_solve_stage(pieces, top_inverse_t):
    n_top, _, rows = top_inverse_t.shape
    width = pieces[0].shape[1]
    n_x = pieces[0].shape[0] // rows

    def body(*refs):
        parts, inverse, out = refs[:CORES], refs[CORES], refs[CORES + 1]
        y, core = lax.axis_index("row") % n_top, lax.axis_index("col") % CORES
        acc = None
        for k, ref in enumerate(parts):
            for x in range(n_x):
                start = pl.multiple_of((x * CORES + (core ^ k)) * rows, rows)
                part = ref[x * rows : (x + 1) * rows, :]
                term = dot(inverse[y, pl.ds(start, rows), :], part, 0)
                acc = term if acc is None else acc + term
        out[...] = acc.astype(BF16)

    return call(body, [(rows, width)], (*pieces, top_inverse_t))[0]


def spread_stage(pieces, n_z, n_top):
    rows, width = pieces[0].shape

    def body(*refs):
        out = refs[len(pieces)]
        row = lax.axis_index("row")
        for k, ref in enumerate(refs[: len(pieces)]):
            z, y = (row ^ k) // n_top, (row ^ k) % n_top
            out[y, :, pl.ds(pl.multiple_of(z * width, width), width)] = ref[...]

    return call(body, [(n_top, rows, n_z * width)], tuple(pieces))[0]


def narrow_spread(pieces, n_z, n_top):
    rows, width = pieces[0].shape
    row = lax.axis_index("row")
    out = jnp.zeros((n_z * n_top, rows, width), BF16)
    for k, piece in enumerate(pieces):
        out = lax.dynamic_update_index_in_dim(out, piece, row ^ k, 0)
    out = out.reshape(n_z, n_top, rows, width).transpose(1, 2, 0, 3)
    return out.reshape(n_top, rows, n_z * width)


def make_local(n_row, n_col):
    n_x = n_col // CORES
    half = n_row // 2

    def row_xor(x, k):
        return lax.ppermute(x, "row", [(i, i ^ k) for i in range(n_row)])

    def col_xor(x, k):
        return lax.ppermute(x, "col", [(i, i ^ k) for i in range(n_col)])

    def local(
        leaf_inverse,
        leaf_rhs,
        leaf_tiles,
        mid_inverse_t,
        mid_rhs,
        mid_tiles,
        top_inverse_t,
        top_rhs,
        tile_lists,
    ):
        nb, _, own_rows = mid_inverse_t.shape
        n_top, _, own_top = top_inverse_t.shape
        src = leaf_rhs.shape[2]
        n_z = n_row // n_top

        solved_leaf, swap, update = leaf_stage(
            leaf_inverse[0], leaf_rhs[0], leaf_tiles[0], tile_lists, mid_inverse_t, mid_tiles, n_row
        )

        crossing, staying = [update[half]], [update[0]]
        for k in reversed(range(1, half)):
            crossing.append(row_xor(update[half + k], k))
        for k in range(1, half):
            staying.append(row_xor(update[k], k))
        summed = cross_stage(crossing, nb, own_rows, src)
        crossed = row_xor(summed, half)
        mine, other = resid_stage(staying, crossed, mid_rhs)

        y = lax.axis_index("row") % nb
        swapped = row_xor(swap, 1)
        share = share_stage(top_rhs, n_z)
        shares = [share] + [col_xor(share, dx * CORES) for dx in range(1, n_x)]

        def up(block, have, by):
            pairs = [(i, i + by * nb) for i in range(have * nb, n_row - by * nb)]
            return lax.ppermute(block, "row", pairs)

        given = row_xor(other, 1)
        blocks = [(mine, given)]
        for away in range(1, n_z):
            by = 2 - away % 2
            blocks.append(tuple(up(b, away - by, by) for b in blocks[away - by]))
        own, other, sent = mid_stage(
            blocks, mid_inverse_t, mid_tiles, swapped, n_x, own_top
        )
        sent = col_xor(sent, 1)
        other_own = row_xor(other, 1)
        mid_own = jnp.where(
            y == 0, jnp.stack([own, other_own]), jnp.stack([other_own, own])
        )

        pieces = list(core_stage(own, other, mid_tiles, swapped, sent, n_z))
        for k in range(1, n_z):
            pieces[k] = row_xor(pieces[k], k * n_top)
        part = sum_stage(pieces)
        parts = [part] + [col_xor(part, dx * CORES) for dx in range(1, n_x)]
        own = top_resid_stage(parts, shares)

        mine = top_solve_stage([own, col_xor(own, 1)], top_inverse_t)
        got = [mine] + [row_xor(mine, k * n_top) for k in range(1, n_z)]
        got = [row_xor(piece, k) if k else piece for piece in got for k in range(n_top)]
        spread = narrow_spread if mine.shape[1] % LANES else spread_stage
        top_own = spread(got, n_z, n_top)
        return solved_leaf[None], mid_own, top_own

    return local


def solution(mesh):
    placed = (
        P(("row", "col"), None, None),
        P(("row", "col"), None, None),
        P(("row", "col"), None, None),
        P("col", None, "row"),
        P("col", "row", None),
        P("col", None, "row"),
        P(None, None, "col"),
        P(None, "col", None),
        P(("row", "col"), None),
    )
    return jax.shard_map(
        make_local(mesh.shape["row"], mesh.shape["col"]),
        mesh=mesh,
        in_specs=placed,
        out_specs=(P(("row", "col"), None, None), P("col", "row", None), P(None, "col", None)),
        check_vma=False,
    )
```

```python
import jax
import jax.numpy as jnp
from jax import lax
from jax.experimental import pallas as pl
from jax.experimental.pallas import tpu as pltpu
from jax.sharding import PartitionSpec as P


CORES = 2
MARK = 16
LANES = 128


F32, BF16 = jnp.float32, jnp.bfloat16
VMEM = pl.BlockSpec(memory_space=pltpu.VMEM)
SMEM = pl.BlockSpec(memory_space=pltpu.SMEM)
HBM = pl.BlockSpec(memory_space=pltpu.HBM)


def wide(x):
    return x.astype(F32)


def total(terms):
    acc = terms[0]
    for term in terms[1:]:
        acc = acc + term
    return acc


def dot(a, b, a_dim):
    return lax.dot_general(a, b, (((a_dim,), (0,)), ((), ())), preferred_element_type=F32)


def in_hbm(x):
    return pltpu.with_memory_space_constraint(x, pltpu.HBM)


def call(body, shapes, args, specs=None, scratch=(), out_specs=None):
    return pl.pallas_call(
        body,
        out_shape=[jax.ShapeDtypeStruct(s, BF16) for s in shapes],
        in_specs=specs or [VMEM] * len(args),
        out_specs=out_specs or [VMEM] * len(shapes),
        scratch_shapes=scratch,
        compiler_params=pltpu.CompilerParams(vmem_limit_bytes=16 << 20),
    )(*args)


def fetch(source, target, sem):
    copy = pltpu.make_async_copy(source, target, sem)
    copy.start()
    return copy


def write_blocks(blocks, update, slot, rows, flip):
    chunks = update.shape[1] // LANES
    mark = jnp.full((MARK, LANES), slot[0, 0].astype(F32), F32).astype(BF16)
    for k, block in enumerate(blocks):
        at = pl.ds(pl.multiple_of((flip ^ k) * rows, rows), rows)
        for j in range(chunks):
            lanes = slice(j * LANES, (j + 1) * LANES)
            block[j * rows : (j + 1) * rows, :] = update[at, lanes]
        block[chunks * rows :, :] = mark


def leaf_stage(leaf_inverse, leaf_rhs, leaf_tiles, tile_lists, n_row):
    depth, src = leaf_rhs.shape
    half = n_row // 2
    rows = depth // n_row
    step = min(256, depth // 2)
    count = depth // step

    def body(inverse_hbm, rhs_hbm, tiles_hbm, slot, solved_hbm, solved, *rest):
        blocks = rest[:half]
        inverse, rhs, tiles, update, sems = rest[half:]
        row = lax.axis_index("row")
        base = (1 - row // half) * (depth // 2)
        spans = [slice(i * step, (i + 1) * step) for i in range(count)]
        first, second, stored = [], [], []
        for i, span in enumerate(spans):
            left = slice(0, (i + 1) * step)
            first.append(fetch(rhs_hbm.at[span], rhs.at[span], sems.at[0, i]))
            first.append(
                fetch(inverse_hbm.at[span, left], inverse.at[span, left], sems.at[1, i])
            )
        for i in range(count // 2):
            at = pl.ds(pl.multiple_of(base + i * step, step), step)
            second.append(fetch(tiles_hbm.at[at], tiles.at[spans[i]], sems.at[2, i]))
        for i, span in enumerate(spans):
            first[2 * i].wait()
            first[2 * i + 1].wait()
            block = dot(inverse[span, : (i + 1) * step], rhs[: (i + 1) * step, :], 1)
            solved[span, :] = block.astype(BF16)
            stored.append(fetch(solved.at[span], solved_hbm.at[span], sems.at[3, i]))
        for i in range(count // 2):
            second[i].wait()
            update[spans[i], :] = dot(tiles[spans[i], :], solved[...], 1).astype(BF16)
        write_blocks(blocks, update, slot, rows, row % half)
        for copy in stored:
            copy.wait()

    out = call(
        body,
        [(depth, src)] * 2 + [(src // LANES * rows + MARK, LANES)] * half,
        (*map(in_hbm, (leaf_inverse, leaf_rhs, leaf_tiles)), tile_lists),
        [HBM, HBM, HBM, SMEM],
        [
            pltpu.VMEM((depth, depth), BF16),
            pltpu.VMEM((depth, src), BF16),
            pltpu.VMEM((depth // 2, depth), BF16),
            pltpu.VMEM((depth // 2, src), BF16),
            pltpu.SemaphoreType.DMA((4, count)),
        ],
        [HBM] + [VMEM] * (half + 1),
    )
    return out[0], out[1], out[2:]


def near_stage(solved, leaf_tiles, tile_lists, mid_inverse_t, mid_tiles, n_row):
    depth, src = solved.shape
    nb, _, own_rows = mid_inverse_t.shape
    half = n_row // 2
    rows = depth // n_row

    def body(solved, tiles_hbm, slot, mid_inverse, mid_tile, swap, *rest):
        blocks, (tiles, update, sems) = rest[:half], rest[half:]
        row = lax.axis_index("row")
        at = pl.ds(pl.multiple_of(row // half * (depth // 2), depth // 2), depth // 2)
        copies = [
            fetch(tiles_hbm.at[at], tiles, sems.at[0]),
            fetch(mid_inverse.at[1 - row % nb], swap.at[0], sems.at[1]),
            fetch(mid_tile.at[1 - row % nb], swap.at[1], sems.at[2]),
        ]
        copies[0].wait()
        update[...] = dot(tiles[...], solved[...], 1).astype(BF16)
        write_blocks(blocks, update, slot, rows, row % half)
        for copy in copies[1:]:
            copy.wait()

    out = call(
        body,
        [(2, depth, own_rows)] + [(src // LANES * rows + MARK, LANES)] * half,
        (solved, in_hbm(leaf_tiles), tile_lists, *map(in_hbm, (mid_inverse_t, mid_tiles))),
        [VMEM, HBM, SMEM, HBM, HBM],
        [
            pltpu.VMEM((depth // 2, depth), BF16),
            pltpu.VMEM((depth // 2, src), BF16),
            pltpu.SemaphoreType.DMA((3,)),
        ],
    )
    return out[0], out[1:]


def slot_sums(blocks, nb, rows, chunk):
    sums = [None] * nb
    for ref in blocks:
        value = wide(ref[chunk * rows : (chunk + 1) * rows, :])
        mark = wide(ref[ref.shape[0] - MARK : ref.shape[0] - MARK + 1, :])
        for s in range(nb):
            term = jnp.where(mark == float(s), value, 0.0)
            sums[s] = term if sums[s] is None else sums[s] + term
    return sums


def by_block(sums, y):
    first, second = sums
    return jnp.where(y == 0, first, second), jnp.where(y == 0, second, first)


def cross_stage(blocks, nb, rows, src):
    def body(*refs):
        mine, other = refs[len(blocks) :]
        y = lax.axis_index("row") % nb
        for j in range(src // LANES):
            lanes = slice(j * LANES, (j + 1) * LANES)
            sums = by_block(slot_sums(refs[: len(blocks)], nb, rows, j), y)
            mine[:, lanes], other[:, lanes] = [value.astype(BF16) for value in sums]

    return call(body, [(rows, src)] * nb, tuple(blocks))


def near_sum_stage(blocks, mid_rhs):
    nb, rows, src = mid_rhs.shape

    def body(*refs):
        near, (rhs, mine, other) = refs[: len(blocks)], refs[len(blocks) :]
        y = lax.axis_index("row") % nb
        for j in range(src // LANES):
            lanes = slice(j * LANES, (j + 1) * LANES)
            sums = slot_sums(near, nb, rows, j)
            terms = by_block([wide(rhs[s, :, lanes]) - sums[s] for s in range(nb)], y)
            mine[:, lanes] = terms[0]
            other[:, lanes] = terms[1].astype(BF16)

    return pl.pallas_call(
        body,
        name="near_sum",
        out_shape=[
            jax.ShapeDtypeStruct((rows, src), F32),
            jax.ShapeDtypeStruct((rows, src), BF16),
        ],
        in_specs=[VMEM] * (len(blocks) + 1),
        out_specs=[VMEM] * 2,
        compiler_params=pltpu.CompilerParams(vmem_limit_bytes=16 << 20),
    )(*blocks, mid_rhs)


def resid_stage(*pairs):
    count = len(pairs)

    def body(*refs):
        for near, far, out in zip(refs[:count], refs[count : 2 * count], refs[2 * count :]):
            out[...] = (wide(near[...]) - wide(far[...])).astype(BF16)

    args = [near for near, _ in pairs] + [far for _, far in pairs]
    return call(body, [pairs[0][1].shape] * count, tuple(args))


def early_stage(blocks, owners, mid_inverse_t, swapped):
    nb, _, rows = mid_inverse_t.shape
    src = blocks[0].shape[1]

    def body(*refs):
        parts, (inverse, swap, out) = refs[: len(blocks)], refs[len(blocks) :]
        out[...] = solve_share(parts, owners, inverse, swap, nb, rows)

    return pl.pallas_call(
        body,
        name="early",
        out_shape=jax.ShapeDtypeStruct((2 * rows, src), F32),
        in_specs=[VMEM] * (len(blocks) + 2),
        out_specs=VMEM,
        compiler_params=pltpu.CompilerParams(vmem_limit_bytes=16 << 20),
    )(*blocks, mid_inverse_t, swapped)


def solve_share(parts, owners, inverse, swap, nb, rows):
    row = lax.axis_index("row")
    z, y = row // nb, row % nb
    acc = None
    for owner, ref in zip(owners, parts):
        at = pl.ds(pl.multiple_of(owner(z, y) * rows, rows), rows)
        part = jnp.concatenate([inverse[y, at, :], swap[0, at, :]], axis=1)
        term = dot(part, ref[...], 0)
        acc = term if acc is None else acc + term
    return acc


def mid_stage(blocks, owners, early, mid_inverse_t, mid_tiles, swapped, n_x, own_top):
    nb, _, rows = mid_inverse_t.shape
    src = blocks[0].shape[1]
    count = len(blocks)

    def body(*refs):
        parts, (start, inverse, tiles, swap, own, other, sent) = refs[:count], refs[count:]
        core = lax.axis_index("col") % CORES
        y = lax.axis_index("row") % nb
        acc = start[...] + solve_share(parts, owners, inverse, swap, nb, rows)
        solved = acc.astype(BF16)
        own[...] = solved[:rows]
        other[...] = solved[rows:]
        for x in range(n_x):
            at = pl.ds(pl.multiple_of((x * CORES + 1 - core) * own_top, own_top), own_top)
            part = jnp.concatenate([tiles[y, at, :], swap[1, at, :]], axis=1)
            sent[x] = dot(part, solved, 1).astype(BF16)

    return call(
        body,
        [(rows, src), (rows, src), (n_x, own_top, src)],
        (*blocks, early, mid_inverse_t, mid_tiles, swapped),
    )


def core_stage(own, other, mid_tiles, swapped, got, n_z):
    n_x, own_top, src = got.shape
    nb = mid_tiles.shape[0]
    width = src // n_z
    dense = width % LANES == 0

    def body(own, other, tiles, swap, far, *rest):
        outs, part = (rest[:-1], rest[-1]) if dense else (None, rest[0])
        row, core = lax.axis_index("row"), lax.axis_index("col") % CORES
        z, y = row // nb, row % nb
        solved = jnp.concatenate([own[...], other[...]], axis=0)
        for x in range(n_x):
            at = pl.ds(pl.multiple_of((x * CORES + core) * own_top, own_top), own_top)
            tile = jnp.concatenate([tiles[y, at, :], swap[1, at, :]], axis=1)
            term = dot(tile, solved, 1) + wide(far[x])
            part[x * own_top : (x + 1) * own_top, :] = term.astype(BF16)
        for k in range(n_z if dense else 0):
            lanes = pl.ds(pl.multiple_of((z ^ k) * width, width), width)
            outs[k][...] = part[:, lanes]

    args = (own, other, mid_tiles, swapped, got)
    rows = n_x * own_top
    if dense:
        return call(body, [(rows, width)] * n_z, args, scratch=[pltpu.VMEM((rows, src), BF16)])
    part = call(body, [(rows, src)], args)[0]
    z = lax.axis_index("row") // nb
    return [lax.dynamic_slice_in_dim(part, (z ^ k) * width, width, 1) for k in range(n_z)]


def share_stage(top_rhs, n_z):
    n_top, rows, src = top_rhs.shape
    width = src // n_z
    row = lax.axis_index("row")
    if width % LANES:
        part = lax.dynamic_index_in_dim(top_rhs, row % n_top, 0, keepdims=False)
        return lax.dynamic_slice_in_dim(part, row // n_top * width, width, 1)

    def body(rhs, out):
        row = lax.axis_index("row")
        lanes = pl.ds(pl.multiple_of(row // n_top * width, width), width)
        out[...] = rhs[row % n_top, :, lanes]

    return call(body, [(rows, width)], (top_rhs,))[0]


def sum_stage(pieces):
    def body(*refs):
        refs[-1][...] = total([wide(ref[...]) for ref in refs[:-1]]).astype(BF16)

    return call(body, [pieces[0].shape], tuple(pieces))[0]


def top_resid_stage(pieces, shares):
    n_x = len(shares)
    rows, width = shares[0].shape

    def body(*refs):
        terms, rhs, out = refs[: len(pieces)], refs[len(pieces) : -1], refs[-1]
        x = lax.axis_index("col") // CORES
        for dx in range(n_x):
            at = pl.ds(pl.multiple_of((x ^ dx) * rows, rows), rows)
            update = total([wide(ref[at, :]) for ref in terms])
            out[at, :] = (wide(rhs[dx][...]) - update).astype(BF16)

    return call(body, [(n_x * rows, width)], (*pieces, *shares))[0]


def top_solve_stage(pieces, top_inverse_t):
    n_top, _, rows = top_inverse_t.shape
    width = pieces[0].shape[1]
    n_x = pieces[0].shape[0] // rows

    def body(*refs):
        parts, inverse, out = refs[:CORES], refs[CORES], refs[CORES + 1]
        y, core = lax.axis_index("row") % n_top, lax.axis_index("col") % CORES
        acc = None
        for k, ref in enumerate(parts):
            for x in range(n_x):
                start = pl.multiple_of((x * CORES + (core ^ k)) * rows, rows)
                part = ref[x * rows : (x + 1) * rows, :]
                term = dot(inverse[y, pl.ds(start, rows), :], part, 0)
                acc = term if acc is None else acc + term
        out[...] = acc.astype(BF16)

    return call(body, [(rows, width)], (*pieces, top_inverse_t))[0]


def spread_stage(pieces, n_z, n_top):
    rows, width = pieces[0].shape
    count = len(pieces)

    def body(*refs):
        out, sems = refs[count:]
        row = lax.axis_index("row")
        copies = []
        for k, ref in enumerate(refs[:count]):
            z, y = (row ^ k) // n_top, (row ^ k) % n_top
            lanes = pl.ds(pl.multiple_of(z * width, width), width)
            copies.append(fetch(ref, out.at[y, :, lanes], sems.at[k]))
        for copy in copies:
            copy.wait()

    return call(
        body,
        [(n_top, rows, n_z * width)],
        tuple(pieces),
        scratch=[pltpu.SemaphoreType.DMA((count,))],
        out_specs=[HBM],
    )[0]


def narrow_spread(pieces, n_z, n_top):
    rows, width = pieces[0].shape
    row = lax.axis_index("row")
    out = jnp.zeros((n_z * n_top, rows, width), BF16)
    for k, piece in enumerate(pieces):
        out = lax.dynamic_update_index_in_dim(out, piece, row ^ k, 0)
    out = out.reshape(n_z, n_top, rows, width).transpose(1, 2, 0, 3)
    return out.reshape(n_top, rows, n_z * width)


def make_local(n_row, n_col):
    n_x = n_col // CORES
    half = n_row // 2

    def row_xor(x, k):
        return lax.ppermute(x, "row", [(i, i ^ k) for i in range(n_row)])

    def col_xor(x, k):
        return lax.ppermute(x, "col", [(i, i ^ k) for i in range(n_col)])

    def local(
        leaf_inverse,
        leaf_rhs,
        leaf_tiles,
        mid_inverse_t,
        mid_rhs,
        mid_tiles,
        top_inverse_t,
        top_rhs,
        tile_lists,
    ):
        nb, _, own_rows = mid_inverse_t.shape
        n_top, _, own_top = top_inverse_t.shape
        src = leaf_rhs.shape[2]
        n_z = n_row // n_top

        solved_leaf, solved, far = leaf_stage(
            leaf_inverse[0], leaf_rhs[0], leaf_tiles[0], tile_lists, n_row
        )
        swap, near = near_stage(
            solved, leaf_tiles[0], tile_lists, mid_inverse_t, mid_tiles, n_row
        )

        crossing, staying = [far[0]], [near[0]]
        for k in range(1, half):
            crossing.append(row_xor(far[k], k))
        for k in range(1, half):
            staying.append(row_xor(near[k], k))
        mine, other = cross_stage(crossing, nb, own_rows, src)
        far_mine = row_xor(mine, half)
        far_given = row_xor(other, half ^ 1)
        near_mine, other = near_sum_stage(staying, mid_rhs)

        y = lax.axis_index("row") % nb
        swapped = row_xor(swap, 1)
        share = share_stage(top_rhs, n_z)
        shares = [share] + [col_xor(share, dx * CORES) for dx in range(1, n_x)]

        def move(block, *hops):
            pairs = [(f * nb + j, t * nb + j) for f, t in hops for j in range(nb)]
            return lax.ppermute(block, "row", pairs)

        near_given = row_xor(other, 1)
        start = resid_stage((near_mine, far_mine), (near_given, far_given))
        blocks, owners = [start], [lambda z: z]
        if n_z == 4:
            z = lax.axis_index("row") // nb
            first, second, third = [], [], []
            for part, b in zip("ab", start):
                first.append(move(b, (0, 2), (2, 3)))
                second.append(move(b, (0, 1), (1, 3)))
            for part, b, f in zip("ab", start, first):
                passed = jnp.where(z == 2, f, b)
                third.append(move(passed, (1, 2), (2, 3)))
            blocks += [first, second, third]
            owners += [
                lambda z: jnp.where(z == 3, 2, 0),
                lambda z: jnp.where(z == 3, 1, 0),
                lambda z: jnp.where(z == 2, 1, 0),
            ]
        else:
            for away in range(1, n_z):
                by = 2 - away % 2
                hops = [(f, f + by) for f in range(away - by, n_z - by)]
                moved = []
                for part, b in zip("ab", blocks[away - by]):
                    moved.append(move(b, *hops))
                blocks.append(moved)
                owners.append(lambda z, away=away: (z - away + n_z) % n_z)
        flat = [b for pair in blocks for b in pair]
        by_row = [
            lambda z, y, owner=owner, k=k: owner(z) * nb + (y ^ k)
            for owner in owners
            for k in range(2)
        ]
        late = [6, 7] if n_z == 4 else [len(flat) - 2, len(flat) - 1]
        soon = [i for i in range(len(flat)) if i not in late]
        early = early_stage(
            [flat[i] for i in soon], [by_row[i] for i in soon], mid_inverse_t, swapped
        )
        own, other, sent = mid_stage(
            [flat[i] for i in late],
            [by_row[i] for i in late],
            early,
            mid_inverse_t,
            mid_tiles,
            swapped,
            n_x,
            own_top,
        )
        sent = col_xor(sent, 1)
        other_own = row_xor(other, 1)
        mid_own = jnp.where(
            y == 0, jnp.stack([own, other_own]), jnp.stack([other_own, own])
        )

        pieces = list(core_stage(own, other, mid_tiles, swapped, sent, n_z))
        for k in range(1, n_z):
            pieces[k] = row_xor(pieces[k], k * n_top)
        part = sum_stage(pieces)
        parts = [part] + [col_xor(part, dx * CORES) for dx in range(1, n_x)]
        own = top_resid_stage(parts, shares)

        mine = top_solve_stage([own, col_xor(own, 1)], top_inverse_t)
        got = [mine]
        for k in range(1, n_z):
            got.append(row_xor(mine, k * n_top))
        spread_to = []
        for piece in got:
            spread_to += [row_xor(piece, k) if k else piece for k in range(n_top)]
        got = spread_to
        spread = narrow_spread if mine.shape[1] % LANES else spread_stage
        top_own = spread(got, n_z, n_top)
        return solved_leaf[None], mid_own, top_own

    return local


def solution(mesh):
    placed = (
        P(("row", "col"), None, None),
        P(("row", "col"), None, None),
        P(("row", "col"), None, None),
        P("col", None, "row"),
        P("col", "row", None),
        P("col", None, "row"),
        P(None, None, "col"),
        P(None, "col", None),
        P(("row", "col"), None),
    )
    return jax.shard_map(
        make_local(mesh.shape["row"], mesh.shape["col"]),
        mesh=mesh,
        in_specs=placed,
        out_specs=(P(("row", "col"), None, None), P("col", "row", None), P(None, "col", None)),
        check_vma=False,
    )
```

```python
import jax
import jax.numpy as jnp
from jax import lax
from jax.experimental import pallas as pl
from jax.experimental.pallas import tpu as pltpu
from jax.sharding import PartitionSpec as P


CORES = 2
MARK = 16
LANES = 128


F32, BF16 = jnp.float32, jnp.bfloat16
VMEM = pl.BlockSpec(memory_space=pltpu.VMEM)
SMEM = pl.BlockSpec(memory_space=pltpu.SMEM)
HBM = pl.BlockSpec(memory_space=pltpu.HBM)


def wide(x):
    return x.astype(F32)


def total(terms):
    acc = terms[0]
    for term in terms[1:]:
        acc = acc + term
    return acc


def dot(a, b, a_dim):
    return lax.dot_general(a, b, (((a_dim,), (0,)), ((), ())), preferred_element_type=F32)


def in_hbm(x):
    return pltpu.with_memory_space_constraint(x, pltpu.HBM)


def call(body, shapes, args, specs=None, scratch=(), out_specs=None):
    return pl.pallas_call(
        body,
        out_shape=[jax.ShapeDtypeStruct(s, BF16) for s in shapes],
        in_specs=specs or [VMEM] * len(args),
        out_specs=out_specs or [VMEM] * len(shapes),
        scratch_shapes=scratch,
        compiler_params=pltpu.CompilerParams(vmem_limit_bytes=16 << 20),
    )(*args)


def fetch(source, target, sem):
    copy = pltpu.make_async_copy(source, target, sem)
    copy.start()
    return copy


def write_blocks(blocks, update, slot, rows, flip):
    chunks = update.shape[1] // LANES
    mark = jnp.full((MARK, LANES), slot[0, 0].astype(F32), F32).astype(BF16)
    for k, block in enumerate(blocks):
        at = pl.ds(pl.multiple_of((flip ^ k) * rows, rows), rows)
        for j in range(chunks):
            lanes = slice(j * LANES, (j + 1) * LANES)
            block[j * rows : (j + 1) * rows, :] = update[at, lanes]
        block[chunks * rows :, :] = mark


def leaf_stage(leaf_inverse, leaf_rhs, leaf_tiles, tile_lists, n_row):
    depth, src = leaf_rhs.shape
    half = n_row // 2
    rows = depth // n_row
    step = min(256, depth // 2)
    count = depth // step

    def body(inverse_hbm, rhs_hbm, tiles_hbm, slot, solved, *rest):
        blocks = rest[:half]
        inverse, rhs, tiles, update, sems = rest[half:]
        row = lax.axis_index("row")
        base = (1 - row // half) * (depth // 2)
        spans = [slice(i * step, (i + 1) * step) for i in range(count)]
        first, second = [], []
        for i, span in enumerate(spans):
            left = slice(0, (i + 1) * step)
            first.append(fetch(rhs_hbm.at[span], rhs.at[span], sems.at[0, i]))
            first.append(
                fetch(inverse_hbm.at[span, left], inverse.at[span, left], sems.at[1, i])
            )
        for i in range(count // 2):
            at = pl.ds(pl.multiple_of(base + i * step, step), step)
            second.append(fetch(tiles_hbm.at[at], tiles.at[spans[i]], sems.at[2, i]))
        for i, span in enumerate(spans):
            first[2 * i].wait()
            first[2 * i + 1].wait()
            block = dot(inverse[span, : (i + 1) * step], rhs[: (i + 1) * step, :], 1)
            solved[span, :] = block.astype(BF16)
        for i in range(count // 2):
            second[i].wait()
            update[spans[i], :] = dot(tiles[spans[i], :], solved[...], 1).astype(BF16)
        write_blocks(blocks, update, slot, rows, row % half)

    out = call(
        body,
        [(depth, src)] + [(src // LANES * rows + MARK, LANES)] * half,
        (*map(in_hbm, (leaf_inverse, leaf_rhs, leaf_tiles)), tile_lists),
        [HBM, HBM, HBM, SMEM],
        [
            pltpu.VMEM((depth, depth), BF16),
            pltpu.VMEM((depth, src), BF16),
            pltpu.VMEM((depth // 2, depth), BF16),
            pltpu.VMEM((depth // 2, src), BF16),
            pltpu.SemaphoreType.DMA((3, count)),
        ],
    )
    return out[0], out[1:]


def near_stage(solved, leaf_tiles, tile_lists, mid_inverse_t, mid_tiles, n_row):
    depth, src = solved.shape
    nb, _, own_rows = mid_inverse_t.shape
    half = n_row // 2
    rows = depth // n_row

    def body(solved, tiles_hbm, slot, mid_inverse, mid_tile, solved_hbm, swap, *rest):
        blocks, (tiles, update, sems) = rest[:half], rest[half:]
        row = lax.axis_index("row")
        at = pl.ds(pl.multiple_of(row // half * (depth // 2), depth // 2), depth // 2)
        copies = [
            fetch(tiles_hbm.at[at], tiles, sems.at[0]),
            fetch(mid_inverse.at[1 - row % nb], swap.at[0], sems.at[1]),
            fetch(mid_tile.at[1 - row % nb], swap.at[1], sems.at[2]),
            fetch(solved, solved_hbm, sems.at[3]),
        ]
        copies[0].wait()
        update[...] = dot(tiles[...], solved[...], 1).astype(BF16)
        write_blocks(blocks, update, slot, rows, row % half)
        for copy in copies[1:]:
            copy.wait()

    out = call(
        body,
        [(depth, src), (2, depth, own_rows)] + [(src // LANES * rows + MARK, LANES)] * half,
        (solved, in_hbm(leaf_tiles), tile_lists, *map(in_hbm, (mid_inverse_t, mid_tiles))),
        [VMEM, HBM, SMEM, HBM, HBM],
        [
            pltpu.VMEM((depth // 2, depth), BF16),
            pltpu.VMEM((depth // 2, src), BF16),
            pltpu.SemaphoreType.DMA((4,)),
        ],
        [HBM] + [VMEM] * (half + 1),
    )
    return out[0], out[1], out[2:]


def slot_sums(blocks, nb, rows, chunk):
    sums = [None] * nb
    for ref in blocks:
        value = wide(ref[chunk * rows : (chunk + 1) * rows, :])
        mark = wide(ref[ref.shape[0] - MARK : ref.shape[0] - MARK + 1, :])
        for s in range(nb):
            term = jnp.where(mark == float(s), value, 0.0)
            sums[s] = term if sums[s] is None else sums[s] + term
    return sums


def by_block(sums, y):
    first, second = sums
    return jnp.where(y == 0, first, second), jnp.where(y == 0, second, first)


def cross_stage(blocks, nb, rows, src):
    def body(*refs):
        mine, other = refs[len(blocks) :]
        y = lax.axis_index("row") % nb
        for j in range(src // LANES):
            lanes = slice(j * LANES, (j + 1) * LANES)
            sums = by_block(slot_sums(refs[: len(blocks)], nb, rows, j), y)
            mine[:, lanes], other[:, lanes] = [value.astype(BF16) for value in sums]

    return call(body, [(rows, src)] * nb, tuple(blocks))


def near_sum_stage(blocks, mid_rhs):
    nb, rows, src = mid_rhs.shape

    def body(*refs):
        near, (rhs, mine, other) = refs[: len(blocks)], refs[len(blocks) :]
        y = lax.axis_index("row") % nb
        for j in range(src // LANES):
            lanes = slice(j * LANES, (j + 1) * LANES)
            sums = slot_sums(near, nb, rows, j)
            terms = by_block([wide(rhs[s, :, lanes]) - sums[s] for s in range(nb)], y)
            mine[:, lanes] = terms[0]
            other[:, lanes] = terms[1].astype(BF16)

    return pl.pallas_call(
        body,
        name="near_sum",
        out_shape=[
            jax.ShapeDtypeStruct((rows, src), F32),
            jax.ShapeDtypeStruct((rows, src), BF16),
        ],
        in_specs=[VMEM] * (len(blocks) + 1),
        out_specs=[VMEM] * 2,
        compiler_params=pltpu.CompilerParams(vmem_limit_bytes=16 << 20),
    )(*blocks, mid_rhs)


def resid_stage(*pairs):
    count = len(pairs)

    def body(*refs):
        for near, far, out in zip(refs[:count], refs[count : 2 * count], refs[2 * count :]):
            out[...] = (wide(near[...]) - wide(far[...])).astype(BF16)

    args = [near for near, _ in pairs] + [far for _, far in pairs]
    return call(body, [pairs[0][1].shape] * count, tuple(args))


def early_stage(blocks, owners, mid_inverse_t, swapped):
    nb, _, rows = mid_inverse_t.shape
    src = blocks[0].shape[1]

    def body(*refs):
        parts, (inverse, swap, out) = refs[: len(blocks)], refs[len(blocks) :]
        out[...] = solve_share(parts, owners, inverse, swap, nb, rows)

    return pl.pallas_call(
        body,
        name="early",
        out_shape=jax.ShapeDtypeStruct((2 * rows, src), F32),
        in_specs=[VMEM] * (len(blocks) + 2),
        out_specs=VMEM,
        compiler_params=pltpu.CompilerParams(vmem_limit_bytes=16 << 20),
    )(*blocks, mid_inverse_t, swapped)


def solve_share(parts, owners, inverse, swap, nb, rows):
    row = lax.axis_index("row")
    z, y = row // nb, row % nb
    acc = None
    for owner, ref in zip(owners, parts):
        at = pl.ds(pl.multiple_of(owner(z, y) * rows, rows), rows)
        part = jnp.concatenate([inverse[y, at, :], swap[0, at, :]], axis=1)
        term = dot(part, ref[...], 0)
        acc = term if acc is None else acc + term
    return acc


def mid_stage(blocks, owners, early, mid_inverse_t, mid_tiles, swapped, n_x, own_top):
    nb, _, rows = mid_inverse_t.shape
    src = blocks[0].shape[1]
    count = len(blocks)

    def body(*refs):
        parts, (start, inverse, tiles, swap, own, other, sent) = refs[:count], refs[count:]
        core = lax.axis_index("col") % CORES
        y = lax.axis_index("row") % nb
        acc = start[...] + solve_share(parts, owners, inverse, swap, nb, rows)
        solved = acc.astype(BF16)
        own[...] = solved[:rows]
        other[...] = solved[rows:]
        for x in range(n_x):
            at = pl.ds(pl.multiple_of((x * CORES + 1 - core) * own_top, own_top), own_top)
            part = jnp.concatenate([tiles[y, at, :], swap[1, at, :]], axis=1)
            sent[x] = dot(part, solved, 1).astype(BF16)

    return call(
        body,
        [(rows, src), (rows, src), (n_x, own_top, src)],
        (*blocks, early, mid_inverse_t, mid_tiles, swapped),
    )


def core_stage(own, other, mid_tiles, swapped, got, n_z):
    n_x, own_top, src = got.shape
    nb = mid_tiles.shape[0]
    width = src // n_z
    dense = width % LANES == 0

    def body(own, other, tiles, swap, far, *rest):
        outs, part = (rest[:-1], rest[-1]) if dense else (None, rest[0])
        row, core = lax.axis_index("row"), lax.axis_index("col") % CORES
        z, y = row // nb, row % nb
        solved = jnp.concatenate([own[...], other[...]], axis=0)
        for x in range(n_x):
            at = pl.ds(pl.multiple_of((x * CORES + core) * own_top, own_top), own_top)
            tile = jnp.concatenate([tiles[y, at, :], swap[1, at, :]], axis=1)
            term = dot(tile, solved, 1) + wide(far[x])
            part[x * own_top : (x + 1) * own_top, :] = term.astype(BF16)
        for k in range(n_z if dense else 0):
            lanes = pl.ds(pl.multiple_of((z ^ k) * width, width), width)
            outs[k][...] = part[:, lanes]

    args = (own, other, mid_tiles, swapped, got)
    rows = n_x * own_top
    if dense:
        return call(body, [(rows, width)] * n_z, args, scratch=[pltpu.VMEM((rows, src), BF16)])
    part = call(body, [(rows, src)], args)[0]
    z = lax.axis_index("row") // nb
    return [lax.dynamic_slice_in_dim(part, (z ^ k) * width, width, 1) for k in range(n_z)]


def share_stage(top_rhs, n_z):
    n_top, rows, src = top_rhs.shape
    width = src // n_z
    row = lax.axis_index("row")
    if width % LANES:
        part = lax.dynamic_index_in_dim(top_rhs, row % n_top, 0, keepdims=False)
        return lax.dynamic_slice_in_dim(part, row // n_top * width, width, 1)

    def body(rhs, out):
        row = lax.axis_index("row")
        lanes = pl.ds(pl.multiple_of(row // n_top * width, width), width)
        out[...] = rhs[row % n_top, :, lanes]

    return call(body, [(rows, width)], (top_rhs,))[0]


def sum_stage(pieces):
    def body(*refs):
        refs[-1][...] = total([wide(ref[...]) for ref in refs[:-1]]).astype(BF16)

    return call(body, [pieces[0].shape], tuple(pieces))[0]


def top_resid_stage(pieces, shares):
    n_x = len(shares)
    rows, width = shares[0].shape

    def body(*refs):
        terms, rhs, out = refs[: len(pieces)], refs[len(pieces) : -1], refs[-1]
        x = lax.axis_index("col") // CORES
        for dx in range(n_x):
            at = pl.ds(pl.multiple_of((x ^ dx) * rows, rows), rows)
            update = total([wide(ref[at, :]) for ref in terms])
            out[at, :] = (wide(rhs[dx][...]) - update).astype(BF16)

    return call(body, [(n_x * rows, width)], (*pieces, *shares))[0]


def top_solve_stage(pieces, top_inverse_t):
    n_top, _, rows = top_inverse_t.shape
    width = pieces[0].shape[1]
    n_x = pieces[0].shape[0] // rows

    def body(*refs):
        parts, inverse, out = refs[:CORES], refs[CORES], refs[CORES + 1]
        y, core = lax.axis_index("row") % n_top, lax.axis_index("col") % CORES
        acc = None
        for k, ref in enumerate(parts):
            for x in range(n_x):
                start = pl.multiple_of((x * CORES + (core ^ k)) * rows, rows)
                part = ref[x * rows : (x + 1) * rows, :]
                term = dot(inverse[y, pl.ds(start, rows), :], part, 0)
                acc = term if acc is None else acc + term
        out[...] = acc.astype(BF16)

    return call(body, [(rows, width)], (*pieces, top_inverse_t))[0]


def spread_stage(pieces, n_z, n_top):
    rows, width = pieces[0].shape
    count = len(pieces)

    def body(*refs):
        out, sems = refs[count:]
        row = lax.axis_index("row")
        copies = []
        for k, ref in enumerate(refs[:count]):
            z, y = (row ^ k) // n_top, (row ^ k) % n_top
            lanes = pl.ds(pl.multiple_of(z * width, width), width)
            copies.append(fetch(ref, out.at[y, :, lanes], sems.at[k]))
        for copy in copies:
            copy.wait()

    return call(
        body,
        [(n_top, rows, n_z * width)],
        tuple(pieces),
        scratch=[pltpu.SemaphoreType.DMA((count,))],
        out_specs=[HBM],
    )[0]


def narrow_spread(pieces, n_z, n_top):
    rows, width = pieces[0].shape
    row = lax.axis_index("row")
    out = jnp.zeros((n_z * n_top, rows, width), BF16)
    for k, piece in enumerate(pieces):
        out = lax.dynamic_update_index_in_dim(out, piece, row ^ k, 0)
    out = out.reshape(n_z, n_top, rows, width).transpose(1, 2, 0, 3)
    return out.reshape(n_top, rows, n_z * width)


def make_local(n_row, n_col):
    n_x = n_col // CORES
    half = n_row // 2

    def row_xor(x, k):
        return lax.ppermute(x, "row", [(i, i ^ k) for i in range(n_row)])

    def col_xor(x, k):
        return lax.ppermute(x, "col", [(i, i ^ k) for i in range(n_col)])

    def local(
        leaf_inverse,
        leaf_rhs,
        leaf_tiles,
        mid_inverse_t,
        mid_rhs,
        mid_tiles,
        top_inverse_t,
        top_rhs,
        tile_lists,
    ):
        nb, _, own_rows = mid_inverse_t.shape
        n_top, _, own_top = top_inverse_t.shape
        src = leaf_rhs.shape[2]
        n_z = n_row // n_top

        solved, far = leaf_stage(
            leaf_inverse[0], leaf_rhs[0], leaf_tiles[0], tile_lists, n_row
        )
        solved_leaf, swap, near = near_stage(
            solved, leaf_tiles[0], tile_lists, mid_inverse_t, mid_tiles, n_row
        )

        crossing, staying = [far[0]], [near[0]]
        for k in range(1, half):
            crossing.append(row_xor(far[k], k))
        for k in range(1, half):
            staying.append(row_xor(near[k], k))
        mine, other = cross_stage(crossing, nb, own_rows, src)
        far_mine = row_xor(mine, half)
        far_given = row_xor(other, half ^ 1)
        near_mine, other = near_sum_stage(staying, mid_rhs)

        y = lax.axis_index("row") % nb
        swapped = row_xor(swap, 1)
        share = share_stage(top_rhs, n_z)
        shares = [share] + [col_xor(share, dx * CORES) for dx in range(1, n_x)]

        def move(block, *hops):
            pairs = [(f * nb + j, t * nb + j) for f, t in hops for j in range(nb)]
            return lax.ppermute(block, "row", pairs)

        near_given = row_xor(other, 1)
        start = (
            *resid_stage((near_mine, far_mine)),
            *resid_stage((near_given, far_given)),
        )
        blocks, owners = [start], [lambda z: z]
        if n_z == 4:
            z = lax.axis_index("row") // nb
            first, second, third = [], [], []
            for part, b in zip("ab", start):
                first.append(move(b, (0, 2), (2, 3)))
                second.append(move(b, (0, 1), (1, 3)))
            for part, b, f in zip("ab", start, first):
                passed = jnp.where(z == 2, f, b)
                third.append(move(passed, (1, 2), (2, 3)))
            blocks += [first, second, third]
            owners += [
                lambda z: jnp.where(z == 3, 2, 0),
                lambda z: jnp.where(z == 3, 1, 0),
                lambda z: jnp.where(z == 2, 1, 0),
            ]
        else:
            for away in range(1, n_z):
                by = 2 - away % 2
                hops = [(f, f + by) for f in range(away - by, n_z - by)]
                moved = []
                for part, b in zip("ab", blocks[away - by]):
                    moved.append(move(b, *hops))
                blocks.append(moved)
                owners.append(lambda z, away=away: (z - away + n_z) % n_z)
        flat = [b for pair in blocks for b in pair]
        by_row = [
            lambda z, y, owner=owner, k=k: owner(z) * nb + (y ^ k)
            for owner in owners
            for k in range(2)
        ]
        late = [6, 7] if n_z == 4 else [len(flat) - 2, len(flat) - 1]
        soon = [i for i in range(len(flat)) if i not in late]
        early = early_stage(
            [flat[i] for i in soon], [by_row[i] for i in soon], mid_inverse_t, swapped
        )
        own, other, sent = mid_stage(
            [flat[i] for i in late],
            [by_row[i] for i in late],
            early,
            mid_inverse_t,
            mid_tiles,
            swapped,
            n_x,
            own_top,
        )
        sent = col_xor(sent, 1)
        other_own = row_xor(other, 1)
        mid_own = jnp.where(
            y == 0, jnp.stack([own, other_own]), jnp.stack([other_own, own])
        )

        pieces = list(core_stage(own, other, mid_tiles, swapped, sent, n_z))
        for k in range(1, n_z):
            pieces[k] = row_xor(pieces[k], k * n_top)
        part = sum_stage(pieces)
        parts = [part] + [col_xor(part, dx * CORES) for dx in range(1, n_x)]
        own = top_resid_stage(parts, shares)

        mine = top_solve_stage([own, col_xor(own, 1)], top_inverse_t)
        got = [mine]
        for k in range(1, n_z):
            got.append(row_xor(mine, k * n_top))
        spread_to = []
        for piece in got:
            spread_to += [row_xor(piece, k) if k else piece for k in range(n_top)]
        got = spread_to
        spread = narrow_spread if mine.shape[1] % LANES else spread_stage
        top_own = spread(got, n_z, n_top)
        return solved_leaf[None], mid_own, top_own

    return local


def solution(mesh):
    placed = (
        P(("row", "col"), None, None),
        P(("row", "col"), None, None),
        P(("row", "col"), None, None),
        P("col", None, "row"),
        P("col", "row", None),
        P("col", None, "row"),
        P(None, None, "col"),
        P(None, "col", None),
        P(("row", "col"), None),
    )
    return jax.shard_map(
        make_local(mesh.shape["row"], mesh.shape["col"]),
        mesh=mesh,
        in_specs=placed,
        out_specs=(P(("row", "col"), None, None), P("col", "row", None), P(None, "col", None)),
        check_vma=False,
    )
```

```python
import jax
import jax.numpy as jnp
from jax import lax
from jax.experimental import pallas as pl
from jax.experimental.pallas import tpu as pltpu
from jax.sharding import PartitionSpec as P


CORES = 2
MARK = 16
LANES = 128


F32, BF16 = jnp.float32, jnp.bfloat16
VMEM = pl.BlockSpec(memory_space=pltpu.VMEM)
SMEM = pl.BlockSpec(memory_space=pltpu.SMEM)
HBM = pl.BlockSpec(memory_space=pltpu.HBM)


def wide(x):
    return x.astype(F32)


def total(terms):
    acc = terms[0]
    for term in terms[1:]:
        acc = acc + term
    return acc


def dot(a, b, a_dim):
    return lax.dot_general(a, b, (((a_dim,), (0,)), ((), ())), preferred_element_type=F32)


def in_hbm(x):
    return pltpu.with_memory_space_constraint(x, pltpu.HBM)


def call(body, shapes, args, specs=None, scratch=(), out_specs=None):
    return pl.pallas_call(
        body,
        out_shape=[jax.ShapeDtypeStruct(s, BF16) for s in shapes],
        in_specs=specs or [VMEM] * len(args),
        out_specs=out_specs or [VMEM] * len(shapes),
        scratch_shapes=scratch,
        compiler_params=pltpu.CompilerParams(vmem_limit_bytes=16 << 20),
    )(*args)


def fetch(source, target, sem):
    copy = pltpu.make_async_copy(source, target, sem)
    copy.start()
    return copy


def write_blocks(blocks, update, slot, rows, flip):
    chunks = update.shape[1] // LANES
    mark = jnp.full((MARK, LANES), slot[0, 0].astype(F32), F32).astype(BF16)
    for k, block in enumerate(blocks):
        at = pl.ds(pl.multiple_of((flip ^ k) * rows, rows), rows)
        for j in range(chunks):
            lanes = slice(j * LANES, (j + 1) * LANES)
            block[j * rows : (j + 1) * rows, :] = update[at, lanes]
        block[chunks * rows :, :] = mark


def leaf_stage(leaf_inverse, leaf_rhs, leaf_tiles, tile_lists, n_row):
    depth, src = leaf_rhs.shape
    half = n_row // 2
    rows = depth // n_row
    step = min(256, depth // 2)
    count = depth // step

    def body(inverse_hbm, rhs_hbm, tiles_hbm, slot, solved, near_tiles, *rest):
        blocks = rest[:half]
        inverse, rhs, tiles, update, sems = rest[half:]
        row = lax.axis_index("row")
        base = (1 - row // half) * (depth // 2)
        spans = [slice(i * step, (i + 1) * step) for i in range(count)]
        first, second = [], []
        for i, span in enumerate(spans):
            left = slice(0, (i + 1) * step)
            first.append(fetch(rhs_hbm.at[span], rhs.at[span], sems.at[0, i]))
            first.append(
                fetch(inverse_hbm.at[span, left], inverse.at[span, left], sems.at[1, i])
            )
        for i in range(count // 2):
            at = pl.ds(pl.multiple_of(base + i * step, step), step)
            second.append(fetch(tiles_hbm.at[at], tiles.at[spans[i]], sems.at[2, i]))
        at = pl.ds(pl.multiple_of(row // half * (depth // 2), depth // 2), depth // 2)
        kept = fetch(tiles_hbm.at[at], near_tiles, sems.at[3, 0])
        for i, span in enumerate(spans):
            first[2 * i].wait()
            first[2 * i + 1].wait()
            block = dot(inverse[span, : (i + 1) * step], rhs[: (i + 1) * step, :], 1)
            solved[span, :] = block.astype(BF16)
        for i in range(count // 2):
            second[i].wait()
            update[spans[i], :] = dot(tiles[spans[i], :], solved[...], 1).astype(BF16)
        write_blocks(blocks, update, slot, rows, row % half)
        kept.wait()

    out = call(
        body,
        [(depth, src), (depth // 2, depth)] + [(src // LANES * rows + MARK, LANES)] * half,
        (*map(in_hbm, (leaf_inverse, leaf_rhs, leaf_tiles)), tile_lists),
        [HBM, HBM, HBM, SMEM],
        [
            pltpu.VMEM((depth, depth), BF16),
            pltpu.VMEM((depth, src), BF16),
            pltpu.VMEM((depth // 2, depth), BF16),
            pltpu.VMEM((depth // 2, src), BF16),
            pltpu.SemaphoreType.DMA((4, count)),
        ],
    )
    return out[0], out[1], out[2:]


def near_stage(solved, near_tiles, tile_lists, mid_inverse_t, mid_tiles, n_row):
    depth, src = solved.shape
    nb, _, own_rows = mid_inverse_t.shape
    half = n_row // 2
    rows = depth // n_row

    def body(solved, tiles, slot, mid_inverse, mid_tile, swap, *rest):
        blocks, (update, sems) = rest[:half], rest[half:]
        row = lax.axis_index("row")
        copies = [
            fetch(source.at[1 - row % nb], swap.at[i], sems.at[i])
            for i, source in enumerate((mid_inverse, mid_tile))
        ]
        update[...] = dot(tiles[...], solved[...], 1).astype(BF16)
        write_blocks(blocks, update, slot, rows, row % half)
        for copy in copies:
            copy.wait()

    out = call(
        body,
        [(2, depth, own_rows)] + [(src // LANES * rows + MARK, LANES)] * half,
        (solved, near_tiles, tile_lists, *map(in_hbm, (mid_inverse_t, mid_tiles))),
        [VMEM, VMEM, SMEM, HBM, HBM],
        [pltpu.VMEM((depth // 2, src), BF16), pltpu.SemaphoreType.DMA((2,))],
    )
    return out[0], out[1:]


def keep_stage(solved):
    def body(solved, out, sem):
        fetch(solved, out, sem.at[0]).wait()

    return call(body, [solved.shape], (solved,), None, [pltpu.SemaphoreType.DMA((1,))], [HBM])[0]


def slot_sums(blocks, nb, rows, chunk):
    sums = [None] * nb
    for ref in blocks:
        value = wide(ref[chunk * rows : (chunk + 1) * rows, :])
        mark = wide(ref[ref.shape[0] - MARK : ref.shape[0] - MARK + 1, :])
        for s in range(nb):
            term = jnp.where(mark == float(s), value, 0.0)
            sums[s] = term if sums[s] is None else sums[s] + term
    return sums


def by_block(sums, y):
    first, second = sums
    return jnp.where(y == 0, first, second), jnp.where(y == 0, second, first)


def cross_stage(blocks, nb, rows, src):
    def body(*refs):
        mine, other = refs[len(blocks) :]
        y = lax.axis_index("row") % nb
        for j in range(src // LANES):
            lanes = slice(j * LANES, (j + 1) * LANES)
            sums = by_block(slot_sums(refs[: len(blocks)], nb, rows, j), y)
            mine[:, lanes], other[:, lanes] = [value.astype(BF16) for value in sums]

    return call(body, [(rows, src)] * nb, tuple(blocks))


def near_sum_stage(blocks, mid_rhs):
    nb, rows, src = mid_rhs.shape

    def body(*refs):
        near, (rhs, mine, other) = refs[: len(blocks)], refs[len(blocks) :]
        y = lax.axis_index("row") % nb
        for j in range(src // LANES):
            lanes = slice(j * LANES, (j + 1) * LANES)
            sums = slot_sums(near, nb, rows, j)
            terms = by_block([wide(rhs[s, :, lanes]) - sums[s] for s in range(nb)], y)
            mine[:, lanes] = terms[0]
            other[:, lanes] = terms[1].astype(BF16)

    return pl.pallas_call(
        body,
        name="near_sum",
        out_shape=[
            jax.ShapeDtypeStruct((rows, src), F32),
            jax.ShapeDtypeStruct((rows, src), BF16),
        ],
        in_specs=[VMEM] * (len(blocks) + 1),
        out_specs=[VMEM] * 2,
        compiler_params=pltpu.CompilerParams(vmem_limit_bytes=16 << 20),
    )(*blocks, mid_rhs)


def resid_stage(*pairs):
    count = len(pairs)

    def body(*refs):
        for near, far, out in zip(refs[:count], refs[count : 2 * count], refs[2 * count :]):
            out[...] = (wide(near[...]) - wide(far[...])).astype(BF16)

    args = [near for near, _ in pairs] + [far for _, far in pairs]
    return call(body, [pairs[0][1].shape] * count, tuple(args))


def early_stage(blocks, owners, mid_inverse_t, swapped):
    nb, _, rows = mid_inverse_t.shape
    src = blocks[0].shape[1]

    def body(*refs):
        parts, (inverse, swap, out) = refs[: len(blocks)], refs[len(blocks) :]
        out[...] = solve_share(parts, owners, inverse, swap, nb, rows)

    return pl.pallas_call(
        body,
        name="early",
        out_shape=jax.ShapeDtypeStruct((2 * rows, src), F32),
        in_specs=[VMEM] * (len(blocks) + 2),
        out_specs=VMEM,
        compiler_params=pltpu.CompilerParams(vmem_limit_bytes=16 << 20),
    )(*blocks, mid_inverse_t, swapped)


def solve_share(parts, owners, inverse, swap, nb, rows):
    row = lax.axis_index("row")
    z, y = row // nb, row % nb
    acc = None
    for owner, ref in zip(owners, parts):
        at = pl.ds(pl.multiple_of(owner(z, y) * rows, rows), rows)
        part = jnp.concatenate([inverse[y, at, :], swap[0, at, :]], axis=1)
        term = dot(part, ref[...], 0)
        acc = term if acc is None else acc + term
    return acc


def mid_stage(blocks, owners, early, mid_inverse_t, mid_tiles, swapped, n_x, own_top):
    nb, _, rows = mid_inverse_t.shape
    src = blocks[0].shape[1]
    count = len(blocks)

    def body(*refs):
        parts, (start, inverse, tiles, swap, own, other, sent) = refs[:count], refs[count:]
        core = lax.axis_index("col") % CORES
        y = lax.axis_index("row") % nb
        acc = start[...] + solve_share(parts, owners, inverse, swap, nb, rows)
        solved = acc.astype(BF16)
        own[...] = solved[:rows]
        other[...] = solved[rows:]
        for x in range(n_x):
            at = pl.ds(pl.multiple_of((x * CORES + 1 - core) * own_top, own_top), own_top)
            part = jnp.concatenate([tiles[y, at, :], swap[1, at, :]], axis=1)
            sent[x] = dot(part, solved, 1).astype(BF16)

    return call(
        body,
        [(rows, src), (rows, src), (n_x, own_top, src)],
        (*blocks, early, mid_inverse_t, mid_tiles, swapped),
    )


def core_stage(own, other, mid_tiles, swapped, got, n_z):
    n_x, own_top, src = got.shape
    nb = mid_tiles.shape[0]
    width = src // n_z
    dense = width % LANES == 0

    def body(own, other, tiles, swap, far, *rest):
        outs, part = (rest[:-1], rest[-1]) if dense else (None, rest[0])
        row, core = lax.axis_index("row"), lax.axis_index("col") % CORES
        z, y = row // nb, row % nb
        solved = jnp.concatenate([own[...], other[...]], axis=0)
        for x in range(n_x):
            at = pl.ds(pl.multiple_of((x * CORES + core) * own_top, own_top), own_top)
            tile = jnp.concatenate([tiles[y, at, :], swap[1, at, :]], axis=1)
            term = dot(tile, solved, 1) + wide(far[x])
            part[x * own_top : (x + 1) * own_top, :] = term.astype(BF16)
        for k in range(n_z if dense else 0):
            lanes = pl.ds(pl.multiple_of((z ^ k) * width, width), width)
            outs[k][...] = part[:, lanes]

    args = (own, other, mid_tiles, swapped, got)
    rows = n_x * own_top
    if dense:
        return call(body, [(rows, width)] * n_z, args, scratch=[pltpu.VMEM((rows, src), BF16)])
    part = call(body, [(rows, src)], args)[0]
    z = lax.axis_index("row") // nb
    return [lax.dynamic_slice_in_dim(part, (z ^ k) * width, width, 1) for k in range(n_z)]


def share_stage(top_rhs, n_z):
    n_top, rows, src = top_rhs.shape
    width = src // n_z
    row = lax.axis_index("row")
    if width % LANES:
        part = lax.dynamic_index_in_dim(top_rhs, row % n_top, 0, keepdims=False)
        return lax.dynamic_slice_in_dim(part, row // n_top * width, width, 1)

    def body(rhs, out):
        row = lax.axis_index("row")
        lanes = pl.ds(pl.multiple_of(row // n_top * width, width), width)
        out[...] = rhs[row % n_top, :, lanes]

    return call(body, [(rows, width)], (top_rhs,))[0]


def sum_stage(pieces):
    def body(*refs):
        refs[-1][...] = total([wide(ref[...]) for ref in refs[:-1]]).astype(BF16)

    return call(body, [pieces[0].shape], tuple(pieces))[0]


def top_resid_stage(pieces, shares):
    n_x = len(shares)
    rows, width = shares[0].shape

    def body(*refs):
        terms, rhs, out = refs[: len(pieces)], refs[len(pieces) : -1], refs[-1]
        x = lax.axis_index("col") // CORES
        for dx in range(n_x):
            at = pl.ds(pl.multiple_of((x ^ dx) * rows, rows), rows)
            update = total([wide(ref[at, :]) for ref in terms])
            out[at, :] = (wide(rhs[dx][...]) - update).astype(BF16)

    return call(body, [(n_x * rows, width)], (*pieces, *shares))[0]


def top_solve_stage(piece, top_inverse_t, which, start=None):
    n_top, _, rows = top_inverse_t.shape
    width = piece.shape[1]
    n_x = piece.shape[0] // rows

    def body(ref, inverse, *rest):
        out = rest[-1]
        y, core = lax.axis_index("row") % n_top, lax.axis_index("col") % CORES
        acc = None if start is None else rest[0][...]
        for x in range(n_x):
            at = pl.multiple_of((x * CORES + (core ^ which)) * rows, rows)
            part = ref[x * rows : (x + 1) * rows, :]
            term = dot(inverse[y, pl.ds(at, rows), :], part, 0)
            acc = term if acc is None else acc + term
        out[...] = acc.astype(out.dtype)

    args = (piece, top_inverse_t) + (() if start is None else (start,))
    return pl.pallas_call(
        body,
        out_shape=jax.ShapeDtypeStruct((rows, width), F32 if start is None else BF16),
        in_specs=[VMEM] * len(args),
        out_specs=VMEM,
        compiler_params=pltpu.CompilerParams(vmem_limit_bytes=16 << 20),
    )(*args)


def spread_stage(pieces, n_z, n_top):
    rows, width = pieces[0].shape
    count = len(pieces)

    def body(*refs):
        out, sems = refs[count:]
        row = lax.axis_index("row")
        copies = []
        for k, ref in enumerate(refs[:count]):
            z, y = (row ^ k) // n_top, (row ^ k) % n_top
            lanes = pl.ds(pl.multiple_of(z * width, width), width)
            copies.append(fetch(ref, out.at[y, :, lanes], sems.at[k]))
        for copy in copies:
            copy.wait()

    return call(
        body,
        [(n_top, rows, n_z * width)],
        tuple(pieces),
        scratch=[pltpu.SemaphoreType.DMA((count,))],
        out_specs=[HBM],
    )[0]


def narrow_spread(pieces, n_z, n_top):
    rows, width = pieces[0].shape
    row = lax.axis_index("row")
    out = jnp.zeros((n_z * n_top, rows, width), BF16)
    for k, piece in enumerate(pieces):
        out = lax.dynamic_update_index_in_dim(out, piece, row ^ k, 0)
    out = out.reshape(n_z, n_top, rows, width).transpose(1, 2, 0, 3)
    return out.reshape(n_top, rows, n_z * width)


def make_local(n_row, n_col):
    n_x = n_col // CORES
    half = n_row // 2

    def row_xor(x, k):
        return lax.ppermute(x, "row", [(i, i ^ k) for i in range(n_row)])

    def col_xor(x, k):
        return lax.ppermute(x, "col", [(i, i ^ k) for i in range(n_col)])

    def local(
        leaf_inverse,
        leaf_rhs,
        leaf_tiles,
        mid_inverse_t,
        mid_rhs,
        mid_tiles,
        top_inverse_t,
        top_rhs,
        tile_lists,
    ):
        nb, _, own_rows = mid_inverse_t.shape
        n_top, _, own_top = top_inverse_t.shape
        src = leaf_rhs.shape[2]
        n_z = n_row // n_top

        solved, near_tiles, far = leaf_stage(
            leaf_inverse[0], leaf_rhs[0], leaf_tiles[0], tile_lists, n_row
        )
        swap, near = near_stage(
            solved, near_tiles, tile_lists, mid_inverse_t, mid_tiles, n_row
        )
        solved_leaf = keep_stage(solved)

        crossing, staying = [far[0]], [near[0]]
        for k in range(1, half):
            crossing.append(row_xor(far[k], k))
        for k in reversed(range(1, half)):
            staying.append(row_xor(near[k], k))
        mine, other = cross_stage(crossing, nb, own_rows, src)
        far_mine = row_xor(mine, half)
        far_given = row_xor(other, half ^ 1)
        near_mine, other = near_sum_stage(staying, mid_rhs)

        y = lax.axis_index("row") % nb
        swapped = row_xor(swap, 1)
        share = share_stage(top_rhs, n_z)
        shares = [share] + [col_xor(share, dx * CORES) for dx in range(1, n_x)]

        def move(block, *hops):
            pairs = [(f * nb + j, t * nb + j) for f, t in hops for j in range(nb)]
            return lax.ppermute(block, "row", pairs)

        near_given = row_xor(other, 1)
        start = (
            *resid_stage((near_mine, far_mine)),
            *resid_stage((near_given, far_given)),
        )
        blocks, owners = [start], [lambda z: z]
        if n_z == 4:
            z = lax.axis_index("row") // nb
            first, second, third = [], [], []
            for part, b in zip("ab", start):
                first.append(move(b, (0, 2), (2, 3)))
                second.append(move(b, (0, 1), (1, 3)))
            for part, b, f in zip("ab", start, first):
                passed = jnp.where(z == 2, f, b)
                third.append(move(passed, (1, 2), (2, 3)))
            blocks += [first, second, third]
            owners += [
                lambda z: jnp.where(z == 3, 2, 0),
                lambda z: jnp.where(z == 3, 1, 0),
                lambda z: jnp.where(z == 2, 1, 0),
            ]
        else:
            for away in range(1, n_z):
                by = 2 - away % 2
                hops = [(f, f + by) for f in range(away - by, n_z - by)]
                moved = []
                for part, b in zip("ab", blocks[away - by]):
                    moved.append(move(b, *hops))
                blocks.append(moved)
                owners.append(lambda z, away=away: (z - away + n_z) % n_z)
        flat = [b for pair in blocks for b in pair]
        by_row = [
            lambda z, y, owner=owner, k=k: owner(z) * nb + (y ^ k)
            for owner in owners
            for k in range(2)
        ]
        late = [6, 7] if n_z == 4 else [len(flat) - 2, len(flat) - 1]
        soon = [i for i in range(len(flat)) if i not in late]
        early = early_stage(
            [flat[i] for i in soon], [by_row[i] for i in soon], mid_inverse_t, swapped
        )
        own, other, sent = mid_stage(
            [flat[i] for i in late],
            [by_row[i] for i in late],
            early,
            mid_inverse_t,
            mid_tiles,
            swapped,
            n_x,
            own_top,
        )
        sent = col_xor(sent, 1)
        other_own = row_xor(other, 1)
        mid_own = jnp.where(
            y == 0, jnp.stack([own, other_own]), jnp.stack([other_own, own])
        )

        pieces = list(core_stage(own, other, mid_tiles, swapped, sent, n_z))
        for k in range(1, n_z):
            pieces[k] = row_xor(pieces[k], k * n_top)
        part = sum_stage(pieces)
        parts = [part] + [col_xor(part, dx * CORES) for dx in range(1, n_x)]
        own = top_resid_stage(parts, shares)

        across = col_xor(own, 1)
        begun = top_solve_stage(own, top_inverse_t, 0)
        mine = top_solve_stage(across, top_inverse_t, 1, begun)
        got = [mine]
        for k in range(1, n_z):
            got.append(row_xor(mine, k * n_top))
        spread_to = []
        for piece in got:
            spread_to += [row_xor(piece, k) if k else piece for k in range(n_top)]
        got = spread_to
        spread = narrow_spread if mine.shape[1] % LANES else spread_stage
        top_own = spread(got, n_z, n_top)
        return solved_leaf[None], mid_own, top_own

    return local


def solution(mesh):
    placed = (
        P(("row", "col"), None, None),
        P(("row", "col"), None, None),
        P(("row", "col"), None, None),
        P("col", None, "row"),
        P("col", "row", None),
        P("col", None, "row"),
        P(None, None, "col"),
        P(None, "col", None),
        P(("row", "col"), None),
    )
    return jax.shard_map(
        make_local(mesh.shape["row"], mesh.shape["col"]),
        mesh=mesh,
        in_specs=placed,
        out_specs=(P(("row", "col"), None, None), P("col", "row", None), P(None, "col", None)),
        check_vma=False,
    )
```
